32 devices in a mesh: gx: 4 (over z), gy: 8 (over y, x, core).
Axes of the slice: x: 2, y: 2, z: 4, core: 2. Of those that a mesh axis runs over, the one named last changes fastest.
Arguments:
- basis: float32 [20, 3, 32, 64, 512], P(None, None, 'gx', 'gy'), may hold values from -8 to 8
- base_flow: float32 [3, 32, 64, 512], P(None, 'gx', 'gy'), may hold values from -6 to 6
Outputs:
- next_vector: float32 [3, 32, 64, 512], P(None, 'gx', 'gy')
- hessenberg: float32 [21], replicated
The draws below stay inside these ranges and needn't reach their ends.
All inputs are finite; a program needn't handle non-finite values.
Results may differ from the reference program's by a relative error of at most 0.005.
Values sent between devices are 32-bit elements; how exact they have to be, the bound alone decides.
A program may use at most 128 MiB of HBM per device.

```python
import math
import jax
import jax.numpy as jnp
import numpy as np
from jax import lax

SWEEPS = 4
BASIS = 20
NX = 32
NY = 64
NZ = 512
N_GX = 4
N_GY = 8


def draw_basis(key, part):
    key_common = jax.random.fold_in(key, 101)
    key_coef = jax.random.fold_in(key, 202)
    key_noise = jax.random.fold_in(key, 303)
    common = jax.random.normal(key_common, (1, 3, NX, NY, NZ), jnp.float32)
    coefs = jax.random.uniform(key_coef, (BASIS, 1, 1, 1, 1), jnp.float32, 0.4, 1.2)
    noise = jax.random.normal(key_noise, (BASIS, 3, NX, NY, NZ), jnp.float32)
    return jnp.clip(coefs * common + noise, -8.0, 8.0)


def levels(own_key, shape, split, smallest, largest):
    loudness = 1.0
    for position, parts in split:
        draws = jax.random.uniform(jax.random.fold_in(jax.random.fold_in(own_key, 6), position), (parts,), jnp.float32, smallest / len(split), largest / len(split))
        loudness = loudness * jnp.repeat(jnp.exp(draws), shape[position] // parts).reshape((-1,) + (1,) * (len(shape) - 1 - position))
    return loudness


def bell_draw(key, dims, deviation, most, cuts=(), kind=jnp.bfloat16):
    values = jax.random.normal(key, dims, jnp.float32) * deviation
    if len(cuts) > 0:
        values = levels(key, dims, cuts, -0.22, 0.18) * values
    return jnp.clip(values, min=-most, max=most).astype(kind)


def setup_inputs(seed: int = 0) -> dict:
    arg_keys = jax.random.split(jax.random.key(seed), 3)
    return {
        "basis": draw_basis(jax.random.fold_in(arg_keys[2], 71), 0),
        "base_flow": bell_draw(arg_keys[1], (3, NX, NY, NZ), 1.0, 6.0, ((1, 4), (2, 8)), jnp.float32),
    }


time_step = 0.02
viscosity = 0.05
pressure_shift = 0.25
relaxation = 0.6
coarse_face = 2.0
coarse_reach = 4.0
norm_eps = 1e-06
inner_a = 0.8717401485096066
inner_b = 0.5917001814331423
inner_c = 0.2092992179024789

def legendre_seven(points):
    before = points * 0.0 + 1.0
    current = points.copy()
    for degree in range(1, 7):
        following = ((2 * degree + 1) * points * current - degree * before) / (degree + 1)
        before = current
        current = following
    return current

def jacobi_eigen(matrix):
    work = matrix.copy()
    vectors = np.eye(8)
    for sweep_idx in range(10):
        for p_idx in range(7):
            for q_idx in range(p_idx + 1, 8):
                off_value = float(work[p_idx, q_idx])
                if abs(off_value) > 1e-300:
                    theta = 0.5 * math.atan2(2.0 * off_value, float(work[p_idx, p_idx] - work[q_idx, q_idx]))
                    cosine = math.cos(theta)
                    sine = math.sin(theta)
                    rotation = np.eye(8)
                    rotation[p_idx, p_idx] = cosine
                    rotation[q_idx, q_idx] = cosine
                    rotation[q_idx, p_idx] = sine
                    rotation[p_idx, q_idx] = -sine
                    work = rotation.T @ work @ rotation
                    vectors = vectors @ rotation
    eigenvalues = np.array([work[row_idx, row_idx] for row_idx in range(8)])
    return (eigenvalues, vectors)

def gll_tables():
    order = 7
    nodes = np.array([-1.0, -inner_a, -inner_b, -inner_c, inner_c, inner_b, inner_a, 1.0])
    node_values = legendre_seven(nodes)
    weights = 2.0 / (order * (order + 1) * node_values ** 2)
    derivative = np.zeros((8, 8))
    for row_idx in range(8):
        for col_idx in range(8):
            if row_idx != col_idx:
                derivative[row_idx, col_idx] = node_values[row_idx] / (node_values[col_idx] * (nodes[row_idx] - nodes[col_idx]))
    derivative[0, 0] = -order * (order + 1) / 4.0
    derivative[7, 7] = order * (order + 1) / 4.0
    stiffness = derivative.T @ (weights[:, None] * derivative)
    scaling = 1.0 / np.sqrt(weights)
    symmetric = scaling[:, None] * stiffness * scaling[None, :]
    symmetric = 0.5 * (symmetric + symmetric.T)
    eigenvalues, vectors = jacobi_eigen(symmetric)
    modes = scaling[:, None] * vectors
    return (weights, derivative, stiffness, eigenvalues, modes)

def cosine_modes(count):
    row_pos = jnp.arange(count, dtype=jnp.float32)[:, None]
    col_pos = jnp.arange(count, dtype=jnp.float32)[None, :]
    scaling = jnp.where(col_pos == 0, jnp.float32(math.sqrt(1.0 / count)), jnp.float32(math.sqrt(2.0 / count)))
    basis_cos = scaling * jnp.cos(math.pi * col_pos * (row_pos + 0.5) / count)
    eigenvalues = 2.0 - 2.0 * jnp.cos(math.pi * jnp.arange(count, dtype=jnp.float32) / count)
    return (basis_cos, eigenvalues)

def along(field_in, matrix, direction):
    components, size_x, size_y, size_z = field_in.shape
    highest = lax.Precision.HIGHEST
    if direction == 1:
        blocks = field_in.reshape(components, size_x // 8, 8, size_y, size_z)
        result = jnp.einsum('ij,cbjyz->cbiyz', matrix, blocks, precision=highest)
    elif direction == 2:
        blocks = field_in.reshape(components, size_x, size_y // 8, 8, size_z)
        result = jnp.einsum('ij,cxbjz->cxbiz', matrix, blocks, precision=highest)
    else:
        blocks = field_in.reshape(components, size_x, size_y, size_z // 8, 8)
        result = jnp.einsum('ij,cxybj->cxybi', matrix, blocks, precision=highest)
    return result.reshape(field_in.shape)

def pair_faces(field_in, direction):
    length = field_in.shape[direction]
    positions = jnp.arange(length)
    zero_plane = jnp.zeros_like(lax.slice_in_dim(field_in, 0, 1, axis=direction))
    following = jnp.concatenate([lax.slice_in_dim(field_in, 1, length, axis=direction), zero_plane], axis=direction)
    preceding = jnp.concatenate([zero_plane, lax.slice_in_dim(field_in, 0, length - 1, axis=direction)], axis=direction)
    mask_shape = tuple((length if dim_pos == direction else 1 for dim_pos in range(4)))
    last_node = (positions % 8 == 7).reshape(mask_shape)
    first_node = (positions % 8 == 0).reshape(mask_shape)
    return field_in + jnp.where(last_node, following, 0.0) + jnp.where(first_node, preceding, 0.0)

def assemble(field_in):
    return pair_faces(pair_faces(pair_faces(field_in, 1), 2), 3)

def edge_count(start, length, total):
    positions = start + jnp.arange(length, dtype=jnp.int32)
    upper_side = (positions % 8 == 7) & (positions < total - 1)
    lower_side = (positions % 8 == 0) & (positions > 0)
    return 1.0 + upper_side.astype(jnp.float32) + lower_side.astype(jnp.float32)

def reference(basis, base_flow):
    weights_np, derivative_np, stiffness_np, eigen_np, modes_np = gll_tables()
    derivative = jnp.asarray(derivative_np, jnp.float32)
    stiffness = jnp.asarray(stiffness_np, jnp.float32)
    modes = jnp.asarray(modes_np, jnp.float32)
    modes_t = jnp.asarray(modes_np.T, jnp.float32)
    weights = jnp.asarray(weights_np, jnp.float32)
    eigen = jnp.asarray(eigen_np, jnp.float32)
    components, size_x, size_y, size_z = base_flow.shape
    elem_z = size_z // 8
    weight_x = jnp.tile(weights, size_x // 8).reshape(1, size_x, 1, 1)
    weight_y = jnp.tile(weights, size_y // 8).reshape(1, 1, size_y, 1)
    weight_z = jnp.tile(weights, elem_z).reshape(1, 1, 1, size_z)
    weight_3 = weight_x * weight_y * weight_z
    eigen_x = jnp.tile(eigen, size_x // 8).reshape(1, size_x, 1, 1)
    eigen_y = jnp.tile(eigen, size_y // 8).reshape(1, 1, size_y, 1)
    eigen_z = jnp.tile(eigen, elem_z).reshape(1, 1, 1, size_z)
    local_denom = eigen_x + eigen_y + eigen_z + pressure_shift
    mult = edge_count(0, size_x, size_x).reshape(1, size_x, 1, 1) * edge_count(0, size_y, size_y).reshape(1, 1, size_y, 1) * edge_count(0, size_z, size_z).reshape(1, 1, 1, size_z)
    mass_w = weight_3 / (mult * 8.0 * (N_GX * N_GY * elem_z))

    def stiff_apply(field_in):
        return weight_y * weight_z * along(field_in, stiffness, 1) + weight_x * weight_z * along(field_in, stiffness, 2) + weight_x * weight_y * along(field_in, stiffness, 3)

    def local_solve(resid):
        spectral = along(along(along(resid, modes_t, 1), modes_t, 2), modes_t, 3) / local_denom
        return along(along(along(spectral, modes, 1), modes, 2), modes, 3)
    modes_y, eig_y = cosine_modes(N_GY)
    modes_z, eig_z = cosine_modes(elem_z)
    coarse_den = coarse_face * (eig_y[:, None] + eig_z[None, :]) + coarse_reach / float(N_GY * N_GY)

    def coarse_solve(resid):
        shares = (resid / mult)[0].reshape(N_GX, 8, N_GY, 8, elem_z, 8).sum(axis=(1, 3, 5))
        spectral = jnp.einsum('im,gij,jn->gmn', modes_y, shares, modes_z, precision=lax.Precision.HIGHEST) / coarse_den
        solved = jnp.einsum('im,gmn,jn->gij', modes_y, spectral, modes_z, precision=lax.Precision.HIGHEST)
        return jnp.repeat(jnp.repeat(jnp.repeat(solved, 8, 0), 8, 1), 8, 2)[None]
    state = assemble(basis[BASIS - 1]) / mult
    conv = jnp.zeros_like(state)
    for direction in range(3):
        conv = conv + base_flow[direction:direction + 1] * along(state, derivative, direction + 1)
        conv = conv + state[direction:direction + 1] * along(base_flow, derivative, direction + 1)
    visc = stiff_apply(state)
    both = assemble(jnp.concatenate([conv, visc], axis=0))
    star = state - time_step * (both[:3] / mult + viscosity * both[3:] / (weight_3 * mult))
    divergence = jnp.zeros_like(state[:1])
    for direction in range(3):
        divergence = divergence + along(star[direction:direction + 1], derivative, direction + 1)
    rhs = -assemble(weight_3 * divergence)
    phi = jnp.zeros_like(rhs)
    for sweep in range(SWEEPS):
        if sweep == 0:
            resid = rhs
        else:
            resid = rhs - assemble(stiff_apply(phi) + pressure_shift * weight_3 * phi)
        phi = phi + relaxation * assemble(local_solve(resid) + coarse_solve(resid)) / mult
    gradient = jnp.concatenate([along(phi, derivative, direction + 1) for direction in range(3)], axis=0)
    advanced = star - assemble(gradient) / mult
    hcol = jnp.einsum('kcxyz,cxyz->k', basis, advanced * mass_w, precision=lax.Precision.HIGHEST)
    remainder = advanced - jnp.einsum('k,kcxyz->cxyz', hcol, basis, precision=lax.Precision.HIGHEST)
    beta = jnp.sqrt(jnp.sum(remainder * remainder * mass_w) + norm_eps)
    return (remainder / beta, jnp.concatenate([hcol, beta[None]]))
```

```python
import functools
import math

import jax
import jax.numpy as jnp
import numpy as np
from jax import lax
from jax.experimental import pallas as pl
from jax.experimental.pallas import tpu as pltpu
from jax.sharding import PartitionSpec as P

SWEEPS = 4
time_step = 0.02
viscosity = 0.05
pressure_shift = 0.25
relaxation = 0.6
coarse_face = 2.0
coarse_reach = 4.0
norm_eps = 1e-06
inner_a = 0.8717401485096066
inner_b = 0.5917001814331423
inner_c = 0.2092992179024789
MESH = pl.DeviceIdType.MESH
DIRS = [(dx, dy) for dx in (-1, 0, 1) for dy in (-1, 0, 1) if (dx, dy) != (0, 0)]


def legendre_seven(points):
    before = points * 0.0 + 1.0
    current = points.copy()
    for degree in range(1, 7):
        following = ((2 * degree + 1) * points * current - degree * before) / (degree + 1)
        before = current
        current = following
    return current


def jacobi_eigen(matrix):
    work = matrix.copy()
    vectors = np.eye(8)
    for sweep_idx in range(10):
        for p_idx in range(7):
            for q_idx in range(p_idx + 1, 8):
                off_value = float(work[p_idx, q_idx])
                if abs(off_value) > 1e-300:
                    theta = 0.5 * math.atan2(
                        2.0 * off_value, float(work[p_idx, p_idx] - work[q_idx, q_idx])
                    )
                    cosine = math.cos(theta)
                    sine = math.sin(theta)
                    rotation = np.eye(8)
                    rotation[p_idx, p_idx] = cosine
                    rotation[q_idx, q_idx] = cosine
                    rotation[q_idx, p_idx] = sine
                    rotation[p_idx, q_idx] = -sine
                    work = rotation.T @ work @ rotation
                    vectors = vectors @ rotation
    eigenvalues = np.array([work[row_idx, row_idx] for row_idx in range(8)])
    return (eigenvalues, vectors)


def gll_tables():
    order = 7
    nodes = np.array([-1.0, -inner_a, -inner_b, -inner_c, inner_c, inner_b, inner_a, 1.0])
    node_values = legendre_seven(nodes)
    weights = 2.0 / (order * (order + 1) * node_values**2)
    derivative = np.zeros((8, 8))
    for row_idx in range(8):
        for col_idx in range(8):
            if row_idx != col_idx:
                derivative[row_idx, col_idx] = node_values[row_idx] / (
                    node_values[col_idx] * (nodes[row_idx] - nodes[col_idx])
                )
    derivative[0, 0] = -order * (order + 1) / 4.0
    derivative[7, 7] = order * (order + 1) / 4.0
    stiffness = derivative.T @ (weights[:, None] * derivative)
    scaling = 1.0 / np.sqrt(weights)
    symmetric = scaling[:, None] * stiffness * scaling[None, :]
    symmetric = 0.5 * (symmetric + symmetric.T)
    eigenvalues, vectors = jacobi_eigen(symmetric)
    modes = scaling[:, None] * vectors
    return (weights, derivative, stiffness, eigenvalues, modes)


def cosine_modes(count):
    row_pos = np.arange(count)[:, None]
    col_pos = np.arange(count)[None, :]
    scaling = np.where(col_pos == 0, math.sqrt(1.0 / count), math.sqrt(2.0 / count))
    basis_cos = scaling * np.cos(math.pi * col_pos * (row_pos + 0.5) / count)
    eigenvalues = 2.0 - 2.0 * np.cos(math.pi * np.arange(count) / count)
    return (basis_cos, eigenvalues)


def build_tables(count_x, count_y, size_z):
    weights, derivative, stiffness, eigen, modes = gll_tables()
    elem_z = size_z // 8
    lanes = -(-elem_z // 128) * 128
    eye = np.eye(8)
    scaled = stiffness / weights[:, None]
    laplace = np.kron(scaled, eye) + np.kron(eye, scaled)
    left = np.concatenate(
        [
            np.kron(derivative, eye),
            np.kron(eye, derivative),
            viscosity * laplace,
            laplace + pressure_shift * np.eye(64),
            np.kron(modes.T, modes.T),
            np.kron(modes, modes),
        ],
        axis=0,
    )
    blocks = np.eye(16)
    right = np.concatenate(
        [
            np.kron(blocks, matrix).T
            for matrix in (derivative, viscosity * scaled, scaled, modes.T, modes)
        ],
        axis=1,
    )
    weight_xy = np.kron(weights, weights)[:, None]
    weight_3 = weight_xy * np.tile(weights, elem_z)[None, :]
    eigen_xy = (eigen[:, None] + eigen[None, :]).reshape(64, 1)
    inverse = 1.0 / (eigen_xy + np.tile(eigen, elem_z)[None, :] + pressure_shift)
    fields = np.stack([weight_3, inverse])
    modes_y, eig_y = cosine_modes(count_y)
    modes_z, eig_z = cosine_modes(elem_z)
    den = coarse_face * (eig_y[:, None] + eig_z[None, :]) + coarse_reach / float(count_y * count_y)
    down = np.zeros((size_z, lanes))
    down[:, :elem_z] = np.repeat(modes_z, 8, axis=0)
    up = np.zeros((lanes, size_z))
    up[:elem_z] = np.repeat(modes_z, 8, axis=0).T
    green = np.zeros((count_y + 2, count_y, lanes))
    green[1:-1, :, :elem_z] = np.einsum("im,jm,mn->ijn", modes_y, modes_y, 1.0 / den)
    spread = np.repeat(green[1:-1, :, None, :], 8, axis=2)
    spread[:, :, 0] += green[:-2]
    spread[:, :, 7] += green[2:]
    return [
        np.asarray(table, np.float32) for table in (left, right, fields, down, up, spread)
    ]


def dot(a, b):
    return jnp.dot(
        a, b, precision=lax.Precision.HIGHEST, preferred_element_type=jnp.float32
    )


def kernel(
    count_x, count_y, size_b, size_z,
    basis_hbm, base_hbm, left, right, fields, down, up, spread_hbm,
    out, hess,
    basis, base, slopes, spread, field, star, phi, source, state,
    xs3, ys3, cs3, xr3, yr3, cr3,
    xs1, ys1, cs1, xr1, yr1, cr1,
    coarse_s, coarse_r, red_s, red_r,
    load_sem, send3, recv3, send1, recv1, csend, crecv, rsend, rrecv,
):
    gx = lax.axis_index("gx")
    gy = lax.axis_index("gy")
    total = count_x * count_y
    me = gx * count_y + gy
    tiles = size_z // 128

    loads = [
        pltpu.make_async_copy(basis_hbm.at[size_b - 1], basis.at[size_b - 1], load_sem.at[0]),
        pltpu.make_async_copy(base_hbm, base, load_sem.at[1]),
        pltpu.make_async_copy(spread_hbm.at[gy], spread, load_sem.at[2]),
        pltpu.make_async_copy(
            basis_hbm.at[pl.ds(0, size_b - 1)], basis.at[pl.ds(0, size_b - 1)], load_sem.at[3]
        ),
    ]
    for load in loads:
        load.start()
    for buffer in (xr3, yr3, cr3, xr1, yr1, cr1, coarse_r):
        buffer[...] = jnp.zeros_like(buffer)

    barrier = pltpu.get_barrier_semaphore()

    def greet(step, carry):
        other = lax.rem(me + step, total)
        pl.semaphore_signal(
            barrier, inc=1, device_id=(other // count_y, lax.rem(other, count_y)),
            device_id_type=MESH,
        )
        return carry

    lax.fori_loop(1, total, greet, 0)

    def there(dx, dy):
        tests = []
        if dx:
            tests.append((gx > 0) if dx < 0 else (gx < count_x - 1))
        if dy:
            tests.append((gy > 0) if dy < 0 else (gy < count_y - 1))
        return tests[0] if len(tests) == 1 else tests[0] & tests[1]

    row = lax.broadcasted_iota(jnp.int32, (64, size_z), 0)
    lane = lax.broadcasted_iota(jnp.int32, (64, size_z), 1)
    upper_z = (lane % 8 == 7) & (lane < size_z - 1)
    lower_z = (lane % 8 == 0) & (lane > 0)

    def halves(test):
        return jnp.where(test, 0.5, 1.0)

    rmult = (
        halves(((row // 8 == 0) & (gx > 0)) | ((row // 8 == 7) & (gx < count_x - 1)))
        * halves(((row % 8 == 0) & (gy > 0)) | ((row % 8 == 7) & (gy < count_y - 1)))
        * halves(upper_z | lower_z)
    )
    weight_3 = fields.at[0]

    def along_z(f):
        after = pltpu.roll(f, size_z - 1, 1)
        before = pltpu.roll(f, 1, 1)
        return f + jnp.where(upper_z, after, 0.0) + jnp.where(lower_z, before, 0.0)

    def by_left(start, stop, f):
        return dot(left[start:stop, :], f)

    def by_right(start, stop, f):
        stacked = jnp.concatenate([f[:, 128 * t : 128 * t + 128] for t in range(tiles)], axis=0)
        product = dot(stacked, right[:, 128 * start : 128 * stop])
        return [
            jnp.concatenate(
                [product[64 * t : 64 * t + 64, 128 * m : 128 * m + 128] for t in range(tiles)],
                axis=1,
            )
            for m in range(stop - start)
        ]

    def buffers(wide):
        if wide:
            return (xs3, ys3, cs3, xr3, yr3, cr3, send3, recv3)
        return (xs1, ys1, cs1, xr1, yr1, cr1, send1, recv1)

    def each_copy(round_idx, wide, verb):
        xs, ys, cs, xr, yr, cr, ss, rs = buffers(wide)
        for pos, (dx, dy) in enumerate(DIRS):
            ox, oy = (dx + 1) // 2, (dy + 1) // 2
            if dy == 0:
                src, dst, got = xs.at[round_idx, ox], xr.at[round_idx, 1 - ox], xr.at[round_idx, ox]
            elif dx == 0:
                src, dst, got = ys.at[round_idx, oy], yr.at[round_idx, 1 - oy], yr.at[round_idx, oy]
            else:
                src = cs.at[round_idx, 2 * ox + oy]
                dst = cr.at[round_idx, 2 * (1 - ox) + 1 - oy]
                got = cr.at[round_idx, 2 * ox + oy]

            @pl.when(there(dx, dy))
            def _():
                if verb == "start":
                    pltpu.make_async_remote_copy(
                        src_ref=src, dst_ref=dst,
                        send_sem=ss.at[round_idx, pos], recv_sem=rs.at[round_idx, 7 - pos],
                        device_id=(gx + dx, gy + dy), device_id_type=MESH,
                    ).start()
                elif verb == "recv":
                    pltpu.make_async_copy(got, got, rs.at[round_idx, pos]).wait()
                else:
                    pltpu.make_async_copy(src, src, ss.at[round_idx, pos]).wait()

    def cut(value):
        return [value[:, 128 * t : 128 * t + 128] for t in range(tiles)]

    def send(values, round_idx, wide):
        xs, ys, cs = buffers(wide)[:3]
        for c, value in enumerate(values):
            value = along_z(value)
            for t, part in enumerate(cut(value)):
                field[c, t] = part
            xs[round_idx, 0, c] = value[0:8]
            xs[round_idx, 1, c] = value[56:64]
            for o in range(2):
                face = jnp.concatenate(
                    [field[c, t, pl.ds(7 * o, 8, stride=8), :] for t in range(tiles)], axis=1
                )
                ys[round_idx, o, c] = face
                cs[round_idx, o, c] = face[0:1]
                cs[round_idx, 2 + o, c] = face[7:8]
        each_copy(round_idx, wide, "start")

    def receive(count, round_idx, wide):
        xr, yr, cr = buffers(wide)[3:6]
        each_copy(round_idx, wide, "recv")
        results = []
        for c in range(count):
            for t in range(tiles):
                lanes = slice(128 * t, 128 * t + 128)
                field[c, t, 0:8, :] += xr[round_idx, 0, c, :, lanes]
                field[c, t, 56:64, :] += xr[round_idx, 1, c, :, lanes]
                for o in range(2):
                    rows = pl.ds(7 * o, 8, stride=8)
                    field[c, t, rows, :] += yr[round_idx, o, c, :, lanes]
                    field[c, t, 7 * o : 7 * o + 1, :] += cr[round_idx, o, c, :, lanes]
                    field[c, t, 56 + 7 * o : 57 + 7 * o, :] += cr[round_idx, 2 + o, c, :, lanes]
            results.append(jnp.concatenate([field[c, t] for t in range(tiles)], axis=1))
        return results

    loads[0].wait()
    first = [basis[size_b - 1, c] for c in range(3)]
    pl.semaphore_wait(barrier, total - 1)
    send(first, 0, True)
    loads[1].wait()
    for c in range(3):
        value = base[c]
        both = by_left(0, 128, value)
        slopes[0, c] = both[:64]
        slopes[1, c] = both[64:]
        slopes[2, c] = by_right(0, 1, value)[0]
    for c, value in enumerate(receive(3, 0, True)):
        state[c] = value * rmult

    sums = []
    for c in range(3):
        value = state[c]
        products = by_left(0, 192, value)
        along, diffuse = by_right(0, 2, value)
        change = products[128:] + diffuse
        for j, slope in enumerate((products[:64], products[64:128], along)):
            change = change + base[j] * slope + state[j] * slopes[j, c]
        sums.append(change)
    send(sums, 1, True)
    for c, value in enumerate(receive(3, 1, True)):
        star[c] = state[c] - time_step * (value * rmult)

    divergence = (
        by_left(0, 64, star[0]) + by_left(64, 128, star[1]) + by_right(0, 1, star[2])[0]
    )
    source[...] = divergence
    loads[2].wait()

    def coarse_copies(sweep):
        for pos, dx in enumerate((-1, 0, 1)):
            def to(step, carry, dx=dx, pos=pos):
                copy = pltpu.make_async_remote_copy(
                    src_ref=coarse_s.at[sweep],
                    dst_ref=coarse_r.at[sweep, 2 - pos, gy],
                    send_sem=csend.at[sweep, pos],
                    recv_sem=crecv.at[sweep, 2 - pos],
                    device_id=(gx + dx, lax.rem(gy + step, count_y)),
                    device_id_type=MESH,
                )
                copy.start()
                return carry

            if dx == 0:
                lax.fori_loop(1, count_y, to, 0)
            else:
                @pl.when(there(dx, 0))
                def _():
                    lax.fori_loop(0, count_y, to, 0)

    def coarse_wait(sweep, sems):
        for pos, dx in enumerate((-1, 0, 1)):
            part = coarse_r.at[sweep, pos]
            if dx == 0:
                part = coarse_r.at[sweep, pos, pl.ds(0, count_y - 1)]
            if dx == 0:
                pltpu.make_async_copy(part, part, sems.at[sweep, pos]).wait()
            else:

                @pl.when(there(dx, 0))
                def _():
                    pltpu.make_async_copy(part, part, sems.at[sweep, pos]).wait()

    for sweep in range(SWEEPS):
        if sweep == 0:
            whole = source[...]
        else:
            pressure = phi[...]
            whole = source[...] + by_left(192, 256, pressure) + by_right(2, 3, pressure)[0]
        send([-weight_3[...] * whole], 2 * sweep, False)
        resid = receive(1, 2 * sweep, False)[0]
        shares = jnp.sum(resid * rmult, axis=0, keepdims=True)
        shares = dot(jnp.broadcast_to(shares, (8, size_z)), down[...])[0:1]
        coarse_s[sweep] = shares
        coarse_copies(sweep)
        coarse_r[sweep, 1, gy] = shares
        local = by_left(256, 320, resid)
        local = by_right(3, 4, local)[0] * fields[1]
        local = by_left(320, 384, local)
        local = by_right(4, 5, local)[0]
        send([local], 2 * sweep + 1, False)
        coarse_wait(sweep, crecv)
        parts = []
        for pos in range(3):
            part = spread[0] * coarse_r[sweep, pos, 0]
            for j in range(1, count_y):
                part = part + spread[j] * coarse_r[sweep, pos, j]
            parts.append(part)
        levels = dot(jnp.concatenate(parts, axis=0), up[...])
        lower, own, upper = levels[0:8], levels[8:16], levels[16:24]
        flat = jnp.concatenate([own + lower] + [own] * 6 + [own + upper], axis=0)
        step_sum = along_z(flat) + receive(1, 2 * sweep + 1, False)[0]
        update = relaxation * step_sum * rmult
        phi[...] = update if sweep == 0 else phi[...] + update

    pressure = phi[...]
    both = by_left(0, 128, pressure)
    send([both[:64], both[64:], by_right(0, 1, pressure)[0]], 2, True)
    for c, value in enumerate(receive(3, 2, True)):
        star[c] = star[c] - value * rmult
    loads[3].wait()
    mass = weight_3[...] * rmult * (1.0 / (8.0 * total * (size_z // 8)))
    phi[...] = mass

    def fold(value):
        return functools.reduce(
            lambda a, b: a + b, [value[:, 128 * t : 128 * t + 128] for t in range(tiles)]
        )

    def products_of(step, sums):
        c, x = step // 8, lax.rem(step, 8)
        rows = pl.ds(pl.multiple_of(8 * x, 8), 8)
        weighted = star[c, rows, :] * phi[rows, :]
        return tuple(
            total_k + fold(basis[k, c, rows, :] * weighted) for k, total_k in enumerate(sums)
        )

    zero = jnp.zeros((8, 128), jnp.float32)
    sums = lax.fori_loop(0, 24, products_of, (zero,) * size_b)
    lane_1 = lax.broadcasted_iota(jnp.int32, (1, 128), 1)

    def all_sum(which, value):
        red_s[which] = value

        def to(step, carry):
            other = lax.rem(me + step, total)
            pltpu.make_async_remote_copy(
                src_ref=red_s.at[which], dst_ref=red_r.at[which, me],
                send_sem=rsend.at[which], recv_sem=rrecv.at[which],
                device_id=(other // count_y, lax.rem(other, count_y)), device_id_type=MESH,
            ).start()
            return carry

        lax.fori_loop(1, total, to, 0)
        red_r[which, me] = value
        part = red_r.at[which, pl.ds(0, total - 1)]
        pltpu.make_async_copy(part, part, rrecv.at[which]).wait()
        return functools.reduce(lambda a, b: a + b, [red_r[which, j] for j in range(total)])

    own = jnp.zeros((1, 128), jnp.float32)
    for k in range(size_b):
        value = jnp.sum(jnp.sum(sums[k], axis=0, keepdims=True), axis=1, keepdims=True)
        own = jnp.where(lane_1 == k, value, own)
    hcol = all_sum(0, own)
    spreads = [
        jnp.broadcast_to(
            jnp.sum(jnp.where(lane_1 == k, hcol, 0.0), axis=1, keepdims=True), (8, 128)
        )
        for k in range(size_b)
    ]

    def remainder_of(step, squares):
        c, x = step // 8, lax.rem(step, 8)
        rows = pl.ds(pl.multiple_of(8 * x, 8), 8)
        for t in range(tiles):
            lanes = slice(128 * t, 128 * t + 128)
            value = star[c, rows, lanes]
            for k in range(size_b):
                value = value - spreads[k] * basis[k, c, rows, lanes]
            star[c, rows, lanes] = value
            squares = squares + value * value * phi[rows, lanes]
        return squares

    squares = lax.fori_loop(0, 24, remainder_of, zero)
    squared = jnp.sum(jnp.sum(squares, axis=0, keepdims=True), axis=1, keepdims=True)
    squared = all_sum(1, jnp.broadcast_to(squared, (1, 128)))
    beta = jnp.sqrt(squared + norm_eps)
    hess[...] = jnp.where(lane_1 == size_b, beta, hcol)
    scale = 1.0 / beta[:, 0:1]
    for c in range(3):
        out[c] = star[c] * scale

    for round_idx in range(3):
        each_copy(round_idx, True, "sent")
    for round_idx in range(2 * SWEEPS):
        each_copy(round_idx, False, "sent")
    for sweep in range(SWEEPS):
        coarse_wait(sweep, csend)
    for which in range(2):
        part = red_r.at[which, pl.ds(0, total - 1)]
        pltpu.make_async_copy(part, part, rsend.at[which]).wait()


def per_device(basis, base_flow):
    size_b = basis.shape[0]
    components, size_x, size_y, size_z = base_flow.shape
    count_x = lax.axis_size("gx")
    count_y = lax.axis_size("gy")
    tables = build_tables(count_x, count_y, size_z)
    lanes = tables[3].shape[1]
    vmem = functools.partial(pltpu.VMEM, dtype=jnp.float32)
    dma = pltpu.SemaphoreType.DMA
    exchange = []
    for rounds, comps in ((3, 3), (2 * SWEEPS, 1)):
        shapes = [
            (rounds, 2, comps, 8, size_z),
            (rounds, 2, comps, 8, size_z),
            (rounds, 4, comps, 1, size_z),
        ]
        exchange += [vmem(shape) for shape in shapes * 2]
    spec_v = pl.BlockSpec(memory_space=pltpu.VMEM)
    spec_any = pl.BlockSpec(memory_space=pl.ANY)
    out, hess = pl.pallas_call(
        functools.partial(kernel, count_x, count_y, size_b, size_z),
        out_shape=(
            jax.ShapeDtypeStruct((3, 64, size_z), jnp.float32),
            jax.ShapeDtypeStruct((1, 128), jnp.float32),
        ),
        in_specs=[spec_any, spec_any] + [spec_v] * 5 + [spec_any],
        out_specs=(spec_v, spec_v),
        scratch_shapes=[
            vmem((size_b, 3, 64, size_z)),
            vmem((3, 64, size_z)),
            vmem((3, 3, 64, size_z)),
            vmem((count_y, 8, lanes)),
            vmem((3, size_z // 128, 64, 128)),
            vmem((3, 64, size_z)),
            vmem((64, size_z)),
            vmem((64, size_z)),
            vmem((3, 64, size_z)),
        ]
        + exchange
        + [
            vmem((SWEEPS, 1, lanes)),
            vmem((SWEEPS, 3, count_y, 1, lanes)),
            vmem((2, 1, 128)),
            vmem((2, count_x * count_y, 1, 128)),
            dma((4,)),
            dma((3, 8)),
            dma((3, 8)),
            dma((2 * SWEEPS, 8)),
            dma((2 * SWEEPS, 8)),
            dma((SWEEPS, 3)),
            dma((SWEEPS, 3)),
            dma((2,)),
            dma((2,)),
        ],
        compiler_params=pltpu.CompilerParams(
            collective_id=0, has_side_effects=True, vmem_limit_bytes=48 * 1024 * 1024
        ),
    )(
        basis.reshape(size_b, 3, 64, size_z),
        base_flow.reshape(3, 64, size_z),
        *[jnp.asarray(table) for table in tables],
    )
    return (out.reshape(base_flow.shape), hess[0, : size_b + 1])


def solution(mesh):
    return jax.shard_map(
        per_device,
        mesh=mesh,
        in_specs=(P(None, None, "gx", "gy", None), P(None, "gx", "gy", None)),
        out_specs=(P(None, "gx", "gy", None), P()),
        check_vma=False,
    )
```

```python
import functools
import math

import jax
import jax.numpy as jnp
import numpy as np
from jax import lax
from jax.experimental import pallas as pl
from jax.experimental.pallas import tpu as pltpu
from jax.sharding import PartitionSpec as P

SWEEPS = 4
time_step = 0.02
viscosity = 0.05
pressure_shift = 0.25
relaxation = 0.6
coarse_face = 2.0
coarse_reach = 4.0
norm_eps = 1e-06
inner_a = 0.8717401485096066
inner_b = 0.5917001814331423
inner_c = 0.2092992179024789
MESH = pl.DeviceIdType.MESH
DIRS = [(dx, dy) for dx in (-1, 0, 1) for dy in (-1, 0, 1) if (dx, dy) != (0, 0)]


def legendre_seven(points):
    before = points * 0.0 + 1.0
    current = points.copy()
    for degree in range(1, 7):
        following = ((2 * degree + 1) * points * current - degree * before) / (degree + 1)
        before = current
        current = following
    return current


def jacobi_eigen(matrix):
    work = matrix.copy()
    vectors = np.eye(8)
    for sweep_idx in range(10):
        for p_idx in range(7):
            for q_idx in range(p_idx + 1, 8):
                off_value = float(work[p_idx, q_idx])
                if abs(off_value) > 1e-300:
                    theta = 0.5 * math.atan2(
                        2.0 * off_value, float(work[p_idx, p_idx] - work[q_idx, q_idx])
                    )
                    cosine = math.cos(theta)
                    sine = math.sin(theta)
                    rotation = np.eye(8)
                    rotation[p_idx, p_idx] = cosine
                    rotation[q_idx, q_idx] = cosine
                    rotation[q_idx, p_idx] = sine
                    rotation[p_idx, q_idx] = -sine
                    work = rotation.T @ work @ rotation
                    vectors = vectors @ rotation
    eigenvalues = np.array([work[row_idx, row_idx] for row_idx in range(8)])
    return (eigenvalues, vectors)


def gll_tables():
    order = 7
    nodes = np.array([-1.0, -inner_a, -inner_b, -inner_c, inner_c, inner_b, inner_a, 1.0])
    node_values = legendre_seven(nodes)
    weights = 2.0 / (order * (order + 1) * node_values**2)
    derivative = np.zeros((8, 8))
    for row_idx in range(8):
        for col_idx in range(8):
            if row_idx != col_idx:
                derivative[row_idx, col_idx] = node_values[row_idx] / (
                    node_values[col_idx] * (nodes[row_idx] - nodes[col_idx])
                )
    derivative[0, 0] = -order * (order + 1) / 4.0
    derivative[7, 7] = order * (order + 1) / 4.0
    stiffness = derivative.T @ (weights[:, None] * derivative)
    scaling = 1.0 / np.sqrt(weights)
    symmetric = scaling[:, None] * stiffness * scaling[None, :]
    symmetric = 0.5 * (symmetric + symmetric.T)
    eigenvalues, vectors = jacobi_eigen(symmetric)
    modes = scaling[:, None] * vectors
    return (weights, derivative, stiffness, eigenvalues, modes)


def cosine_modes(count):
    row_pos = np.arange(count)[:, None]
    col_pos = np.arange(count)[None, :]
    scaling = np.where(col_pos == 0, math.sqrt(1.0 / count), math.sqrt(2.0 / count))
    basis_cos = scaling * np.cos(math.pi * col_pos * (row_pos + 0.5) / count)
    eigenvalues = 2.0 - 2.0 * np.cos(math.pi * np.arange(count) / count)
    return (basis_cos, eigenvalues)


def halved(table):
    high = table.astype(jnp.bfloat16)
    return high, (table - high.astype(np.float64)).astype(jnp.bfloat16)


def build_tables(count_x, count_y, size_z):
    weights, derivative, stiffness, eigen, modes = gll_tables()
    elem_z = size_z // 8
    lanes = -(-elem_z // 128) * 128
    eye = np.eye(8)
    scaled = stiffness / weights[:, None]
    laplace = np.kron(scaled, eye) + np.kron(eye, scaled)
    left = np.concatenate(
        [
            np.kron(derivative, eye),
            np.kron(eye, derivative),
            viscosity * laplace,
            laplace + pressure_shift * np.eye(64),
            np.kron(modes.T, modes.T),
            np.kron(modes, modes),
        ],
        axis=0,
    )
    blocks = np.eye(16)
    right = np.concatenate(
        [
            np.kron(blocks, matrix).T
            for matrix in (derivative, viscosity * scaled, scaled, modes.T, modes)
        ],
        axis=1,
    )
    weight_xy = np.kron(weights, weights)[:, None]
    weight_3 = weight_xy * np.tile(weights, elem_z)[None, :]
    eigen_xy = (eigen[:, None] + eigen[None, :]).reshape(64, 1)
    inverse = 1.0 / (eigen_xy + np.tile(eigen, elem_z)[None, :] + pressure_shift)
    fields = np.stack([weight_3, inverse])
    modes_y, eig_y = cosine_modes(count_y)
    modes_z, eig_z = cosine_modes(elem_z)
    den = coarse_face * (eig_y[:, None] + eig_z[None, :]) + coarse_reach / float(count_y * count_y)
    down = np.zeros((size_z, lanes))
    down[:, :elem_z] = np.repeat(modes_z, 8, axis=0)
    up = np.zeros((lanes, size_z))
    up[:elem_z] = np.repeat(modes_z, 8, axis=0).T
    green = np.zeros((count_y + 2, count_y, lanes))
    green[1:-1, :, :elem_z] = np.einsum("im,jm,mn->ijn", modes_y, modes_y, 1.0 / den)
    spread = np.repeat(green[1:-1, :, None, :], 8, axis=2)
    spread[:, :, 0] += green[:-2]
    spread[:, :, 7] += green[2:]
    left_hi, left_lo = halved(left)
    right_hi, right_lo = halved(right)
    up_hi, up_lo = halved(up)
    return [
        np.concatenate([left_hi, left_hi, left_lo], axis=1),
        np.concatenate([right_hi, right_hi, right_lo], axis=0),
        np.asarray(fields, np.float32),
        np.concatenate(halved(down), axis=1),
        np.concatenate([up_hi, up_hi, up_lo], axis=0),
        np.asarray(spread, np.float32),
    ]


def split(value):
    high = value.astype(jnp.bfloat16)
    return high, (value - high.astype(jnp.float32)).astype(jnp.bfloat16)


def dot(a, b):
    return jnp.dot(a, b, preferred_element_type=jnp.float32)


def kernel(
    count_x, count_y, size_b, size_z,
    basis_hbm, base_hbm, left_hbm, right_hbm, fields_hbm, down_hbm, up_hbm, spread_hbm,
    out, hess,
    basis, base, left, right, fields, down, up, slopes, spread, field, star, phi, source, state,
    xs3, ys3, cs3, xr3, yr3, cr3,
    xs1, ys1, cs1, xr1, yr1, cr1,
    coarse_s, coarse_r, red_s, red_r,
    load_sem, send3, recv3, send1, recv1, csend, crecv, rsend, rrecv,
):
    gx = lax.axis_index("gx")
    gy = lax.axis_index("gy")
    total = count_x * count_y
    me = gx * count_y + gy
    tiles = size_z // 128
    width = coarse_s.shape[-1]

    loads = [
        pltpu.make_async_copy(basis_hbm.at[size_b - 1], basis.at[size_b - 1], load_sem.at[0]),
        pltpu.make_async_copy(base_hbm, base, load_sem.at[1]),
        pltpu.make_async_copy(spread_hbm.at[gy], spread, load_sem.at[2]),
        pltpu.make_async_copy(
            basis_hbm.at[pl.ds(0, size_b - 1)], basis.at[pl.ds(0, size_b - 1)], load_sem.at[3]
        ),
        pltpu.make_async_copy(left_hbm, left, load_sem.at[4]),
        pltpu.make_async_copy(right_hbm, right, load_sem.at[5]),
        pltpu.make_async_copy(fields_hbm, fields, load_sem.at[6]),
        pltpu.make_async_copy(down_hbm, down, load_sem.at[7]),
        pltpu.make_async_copy(up_hbm, up, load_sem.at[8]),
    ]
    for pos in (0, 1, 4, 5, 2, 6, 7, 8):
        loads[pos].start()
    for buffer in (xr3, yr3, cr3, xr1, yr1, cr1, coarse_r):
        buffer[...] = jnp.zeros_like(buffer)

    barrier = pltpu.get_barrier_semaphore()

    def greet(step, carry):
        other = lax.rem(me + step, total)
        pl.semaphore_signal(
            barrier, inc=1, device_id=(other // count_y, lax.rem(other, count_y)),
            device_id_type=MESH,
        )
        return carry

    lax.fori_loop(1, total, greet, 0)

    def there(dx, dy):
        tests = []
        if dx:
            tests.append((gx > 0) if dx < 0 else (gx < count_x - 1))
        if dy:
            tests.append((gy > 0) if dy < 0 else (gy < count_y - 1))
        return tests[0] if len(tests) == 1 else tests[0] & tests[1]

    row = lax.broadcasted_iota(jnp.int32, (64, size_z), 0)
    lane = lax.broadcasted_iota(jnp.int32, (64, size_z), 1)
    upper_z = (lane % 8 == 7) & (lane < size_z - 1)
    lower_z = (lane % 8 == 0) & (lane > 0)

    def halves(test):
        return jnp.where(test, 0.5, 1.0)

    rmult = (
        halves(((row // 8 == 0) & (gx > 0)) | ((row // 8 == 7) & (gx < count_x - 1)))
        * halves(((row % 8 == 0) & (gy > 0)) | ((row % 8 == 7) & (gy < count_y - 1)))
        * halves(upper_z | lower_z)
    )
    weight_3 = fields.at[0]

    def along_z(f):
        after = pltpu.roll(f, size_z - 1, 1)
        before = pltpu.roll(f, 1, 1)
        return f + jnp.where(upper_z, after, 0.0) + jnp.where(lower_z, before, 0.0)

    def by_left(start, stop, f):
        high, low = split(f)
        return dot(left[start:stop, :], jnp.concatenate([high, low, high], axis=0))

    def by_right(start, stop, f):
        stacked = jnp.concatenate([f[:, 128 * t : 128 * t + 128] for t in range(tiles)], axis=0)
        high, low = split(stacked)
        product = dot(
            jnp.concatenate([high, low, high], axis=1), right[:, 128 * start : 128 * stop]
        )
        return [
            jnp.concatenate(
                [product[64 * t : 64 * t + 64, 128 * m : 128 * m + 128] for t in range(tiles)],
                axis=1,
            )
            for m in range(stop - start)
        ]

    def buffers(wide):
        if wide:
            return (xs3, ys3, cs3, xr3, yr3, cr3, send3, recv3)
        return (xs1, ys1, cs1, xr1, yr1, cr1, send1, recv1)

    def each_copy(round_idx, wide, verb):
        xs, ys, cs, xr, yr, cr, ss, rs = buffers(wide)
        for pos, (dx, dy) in enumerate(DIRS):
            ox, oy = (dx + 1) // 2, (dy + 1) // 2
            if dy == 0:
                src, dst, got = xs.at[round_idx, ox], xr.at[round_idx, 1 - ox], xr.at[round_idx, ox]
            elif dx == 0:
                src, dst, got = ys.at[round_idx, oy], yr.at[round_idx, 1 - oy], yr.at[round_idx, oy]
            else:
                src = cs.at[round_idx, 2 * ox + oy]
                dst = cr.at[round_idx, 2 * (1 - ox) + 1 - oy]
                got = cr.at[round_idx, 2 * ox + oy]

            @pl.when(there(dx, dy))
            def _():
                if verb == "start":
                    pltpu.make_async_remote_copy(
                        src_ref=src, dst_ref=dst,
                        send_sem=ss.at[round_idx, pos], recv_sem=rs.at[round_idx, 7 - pos],
                        device_id=(gx + dx, gy + dy), device_id_type=MESH,
                    ).start()
                elif verb == "recv":
                    pltpu.make_async_copy(got, got, rs.at[round_idx, pos]).wait()
                else:
                    pltpu.make_async_copy(src, src, ss.at[round_idx, pos]).wait()

    def cut(value):
        return [value[:, 128 * t : 128 * t + 128] for t in range(tiles)]

    def send(values, round_idx, wide):
        xs, ys, cs = buffers(wide)[:3]
        for c, value in enumerate(values):
            value = along_z(value)
            for t, part in enumerate(cut(value)):
                field[c, t] = part
            xs[round_idx, 0, c] = value[0:8]
            xs[round_idx, 1, c] = value[56:64]
            for o in range(2):
                face = jnp.concatenate(
                    [field[c, t, pl.ds(7 * o, 8, stride=8), :] for t in range(tiles)], axis=1
                )
                ys[round_idx, o, c] = face
                cs[round_idx, o, c] = face[0:1]
                cs[round_idx, 2 + o, c] = face[7:8]
        each_copy(round_idx, wide, "start")

    def receive(count, round_idx, wide):
        xr, yr, cr = buffers(wide)[3:6]
        each_copy(round_idx, wide, "recv")
        results = []
        for c in range(count):
            for t in range(tiles):
                lanes = slice(128 * t, 128 * t + 128)
                field[c, t, 0:8, :] += xr[round_idx, 0, c, :, lanes]
                field[c, t, 56:64, :] += xr[round_idx, 1, c, :, lanes]
                for o in range(2):
                    rows = pl.ds(7 * o, 8, stride=8)
                    field[c, t, rows, :] += yr[round_idx, o, c, :, lanes]
                    field[c, t, 7 * o : 7 * o + 1, :] += cr[round_idx, o, c, :, lanes]
                    field[c, t, 56 + 7 * o : 57 + 7 * o, :] += cr[round_idx, 2 + o, c, :, lanes]
            results.append(jnp.concatenate([field[c, t] for t in range(tiles)], axis=1))
        return results

    loads[0].wait()
    first = [basis[size_b - 1, c] for c in range(3)]
    pl.semaphore_wait(barrier, total - 1)
    send(first, 0, True)
    loads[3].start()
    for pos in (1, 4, 5):
        loads[pos].wait()
    for c in range(3):
        value = base[c]
        both = by_left(0, 128, value)
        slopes[0, c] = both[:64]
        slopes[1, c] = both[64:]
        slopes[2, c] = by_right(0, 1, value)[0]
    for c, value in enumerate(receive(3, 0, True)):
        state[c] = value * rmult

    sums = []
    for c in range(3):
        value = state[c]
        products = by_left(0, 192, value)
        along, diffuse = by_right(0, 2, value)
        change = products[128:] + diffuse
        for j, slope in enumerate((products[:64], products[64:128], along)):
            change = change + base[j] * slope + state[j] * slopes[j, c]
        sums.append(change)
    send(sums, 1, True)
    for c, value in enumerate(receive(3, 1, True)):
        star[c] = state[c] - time_step * (value * rmult)

    divergence = (
        by_left(0, 64, star[0]) + by_left(64, 128, star[1]) + by_right(0, 1, star[2])[0]
    )
    source[...] = divergence
    for pos in (2, 6, 7, 8):
        loads[pos].wait()

    def coarse_copies(sweep):
        for pos, dx in enumerate((-1, 0, 1)):
            def to(step, carry, dx=dx, pos=pos):
                copy = pltpu.make_async_remote_copy(
                    src_ref=coarse_s.at[sweep],
                    dst_ref=coarse_r.at[sweep, 2 - pos, gy],
                    send_sem=csend.at[sweep, pos],
                    recv_sem=crecv.at[sweep, 2 - pos],
                    device_id=(gx + dx, lax.rem(gy + step, count_y)),
                    device_id_type=MESH,
                )
                copy.start()
                return carry

            if dx == 0:
                lax.fori_loop(1, count_y, to, 0)
            else:
                @pl.when(there(dx, 0))
                def _():
                    lax.fori_loop(0, count_y, to, 0)

    def coarse_wait(sweep, sems):
        for pos, dx in enumerate((-1, 0, 1)):
            part = coarse_r.at[sweep, pos]
            if dx == 0:
                part = coarse_r.at[sweep, pos, pl.ds(0, count_y - 1)]
            if dx == 0:
                pltpu.make_async_copy(part, part, sems.at[sweep, pos]).wait()
            else:

                @pl.when(there(dx, 0))
                def _():
                    pltpu.make_async_copy(part, part, sems.at[sweep, pos]).wait()

    for sweep in range(SWEEPS):
        if sweep == 0:
            whole = source[...]
        else:
            pressure = phi[...]
            whole = source[...] + by_left(192, 256, pressure) + by_right(2, 3, pressure)[0]
        send([-weight_3[...] * whole], 2 * sweep, False)
        resid = receive(1, 2 * sweep, False)[0]
        shares = functools.reduce(
            lambda a, b: a + b, [(resid * rmult)[8 * j : 8 * j + 8] for j in range(8)]
        )
        shares = dot(jnp.concatenate(split(shares), axis=0), down[...])
        shares = jnp.sum(
            shares[0:8, :width] + shares[8:16, :width] + shares[0:8, width:],
            axis=0, keepdims=True,
        )
        coarse_s[sweep] = shares
        coarse_copies(sweep)
        coarse_r[sweep, 1, gy] = shares
        local = by_left(256, 320, resid)
        local = by_right(3, 4, local)[0] * fields[1]
        local = by_left(320, 384, local)
        local = by_right(4, 5, local)[0]
        send([local], 2 * sweep + 1, False)
        coarse_wait(sweep, crecv)
        parts = []
        for pos in range(3):
            part = spread[0] * coarse_r[sweep, pos, 0]
            for j in range(1, count_y):
                part = part + spread[j] * coarse_r[sweep, pos, j]
            parts.append(part)
        high, low = split(jnp.concatenate(parts, axis=0))
        levels = dot(jnp.concatenate([high, low, high], axis=1), up[...])
        lower, own, upper = levels[0:8], levels[8:16], levels[16:24]
        flat = jnp.concatenate([own + lower] + [own] * 6 + [own + upper], axis=0)
        step_sum = along_z(flat) + receive(1, 2 * sweep + 1, False)[0]
        update = relaxation * step_sum * rmult
        phi[...] = update if sweep == 0 else phi[...] + update

    pressure = phi[...]
    both = by_left(0, 128, pressure)
    send([both[:64], both[64:], by_right(0, 1, pressure)[0]], 2, True)
    for c, value in enumerate(receive(3, 2, True)):
        star[c] = star[c] - value * rmult
    loads[3].wait()
    mass = weight_3[...] * rmult * (1.0 / (8.0 * total * (size_z // 8)))
    phi[...] = mass

    def fold(value):
        return functools.reduce(
            lambda a, b: a + b, [value[:, 128 * t : 128 * t + 128] for t in range(tiles)]
        )

    def products_of(step, sums):
        c, x = step // 8, lax.rem(step, 8)
        rows = pl.ds(pl.multiple_of(8 * x, 8), 8)
        weighted = star[c, rows, :] * phi[rows, :]
        return tuple(
            total_k + fold(basis[k, c, rows, :] * weighted) for k, total_k in enumerate(sums)
        )

    zero = jnp.zeros((8, 128), jnp.float32)
    sums = lax.fori_loop(0, 24, products_of, (zero,) * size_b)
    lane_1 = lax.broadcasted_iota(jnp.int32, (1, 128), 1)

    def all_sum(which, value):
        red_s[which] = value

        def to(step, carry):
            other = lax.rem(me + step, total)
            pltpu.make_async_remote_copy(
                src_ref=red_s.at[which], dst_ref=red_r.at[which, me],
                send_sem=rsend.at[which], recv_sem=rrecv.at[which],
                device_id=(other // count_y, lax.rem(other, count_y)), device_id_type=MESH,
            ).start()
            return carry

        lax.fori_loop(1, total, to, 0)
        red_r[which, me] = value
        part = red_r.at[which, pl.ds(0, total - 1)]
        pltpu.make_async_copy(part, part, rrecv.at[which]).wait()
        return functools.reduce(lambda a, b: a + b, [red_r[which, j] for j in range(total)])

    own = jnp.zeros((1, 128), jnp.float32)
    for k in range(size_b):
        value = jnp.sum(jnp.sum(sums[k], axis=0, keepdims=True), axis=1, keepdims=True)
        own = jnp.where(lane_1 == k, value, own)
    hcol = all_sum(0, own)
    spreads = [
        jnp.broadcast_to(
            jnp.sum(jnp.where(lane_1 == k, hcol, 0.0), axis=1, keepdims=True), (8, 128)
        )
        for k in range(size_b)
    ]

    def remainder_of(step, squares):
        c, x = step // 8, lax.rem(step, 8)
        rows = pl.ds(pl.multiple_of(8 * x, 8), 8)
        for t in range(tiles):
            lanes = slice(128 * t, 128 * t + 128)
            value = star[c, rows, lanes]
            for k in range(size_b):
                value = value - spreads[k] * basis[k, c, rows, lanes]
            star[c, rows, lanes] = value
            squares = squares + value * value * phi[rows, lanes]
        return squares

    squares = lax.fori_loop(0, 24, remainder_of, zero)
    squared = jnp.sum(jnp.sum(squares, axis=0, keepdims=True), axis=1, keepdims=True)
    squared = all_sum(1, jnp.broadcast_to(squared, (1, 128)))
    beta = jnp.sqrt(squared + norm_eps)
    hess[...] = jnp.where(lane_1 == size_b, beta, hcol)
    scale = 1.0 / beta[:, 0:1]
    for c in range(3):
        out[c] = star[c] * scale

    for round_idx in range(3):
        each_copy(round_idx, True, "sent")
    for round_idx in range(2 * SWEEPS):
        each_copy(round_idx, False, "sent")
    for sweep in range(SWEEPS):
        coarse_wait(sweep, csend)
    for which in range(2):
        part = red_r.at[which, pl.ds(0, total - 1)]
        pltpu.make_async_copy(part, part, rsend.at[which]).wait()


def per_device(basis, base_flow):
    size_b = basis.shape[0]
    components, size_x, size_y, size_z = base_flow.shape
    count_x = lax.axis_size("gx")
    count_y = lax.axis_size("gy")
    tables = build_tables(count_x, count_y, size_z)
    lanes = tables[5].shape[3]
    vmem = functools.partial(pltpu.VMEM, dtype=jnp.float32)
    dma = pltpu.SemaphoreType.DMA
    exchange = []
    for rounds, comps in ((3, 3), (2 * SWEEPS, 1)):
        shapes = [
            (rounds, 2, comps, 8, size_z),
            (rounds, 2, comps, 8, size_z),
            (rounds, 4, comps, 1, size_z),
        ]
        exchange += [vmem(shape) for shape in shapes * 2]
    spec_v = pl.BlockSpec(memory_space=pltpu.VMEM)
    spec_any = pl.BlockSpec(memory_space=pl.ANY)
    out, hess = pl.pallas_call(
        functools.partial(kernel, count_x, count_y, size_b, size_z),
        out_shape=(
            jax.ShapeDtypeStruct((3, 64, size_z), jnp.float32),
            jax.ShapeDtypeStruct((1, 128), jnp.float32),
        ),
        in_specs=[spec_any] * 8,
        out_specs=(spec_v, spec_v),
        scratch_shapes=[
            vmem((size_b, 3, 64, size_z)),
            vmem((3, 64, size_z)),
        ]
        + [pltpu.VMEM(table.shape, table.dtype) for table in tables[:5]]
        + [
            vmem((3, 3, 64, size_z)),
            vmem((count_y, 8, lanes)),
            vmem((3, size_z // 128, 64, 128)),
            vmem((3, 64, size_z)),
            vmem((64, size_z)),
            vmem((64, size_z)),
            vmem((3, 64, size_z)),
        ]
        + exchange
        + [
            vmem((SWEEPS, 1, lanes)),
            vmem((SWEEPS, 3, count_y, 1, lanes)),
            vmem((2, 1, 128)),
            vmem((2, count_x * count_y, 1, 128)),
            dma((9,)),
            dma((3, 8)),
            dma((3, 8)),
            dma((2 * SWEEPS, 8)),
            dma((2 * SWEEPS, 8)),
            dma((SWEEPS, 3)),
            dma((SWEEPS, 3)),
            dma((2,)),
            dma((2,)),
        ],
        compiler_params=pltpu.CompilerParams(
            collective_id=0, has_side_effects=True, vmem_limit_bytes=60 * 1024 * 1024
        ),
    )(
        basis.reshape(size_b, 3, 64, size_z),
        base_flow.reshape(3, 64, size_z),
        *[jnp.asarray(table) for table in tables],
    )
    return (out.reshape(base_flow.shape), hess[0, : size_b + 1])


def solution(mesh):
    return jax.shard_map(
        per_device,
        mesh=mesh,
        in_specs=(P(None, None, "gx", "gy", None), P(None, "gx", "gy", None)),
        out_specs=(P(None, "gx", "gy", None), P()),
        check_vma=False,
    )
```

```python
import functools
import math

import jax
import jax.numpy as jnp
import numpy as np
from jax import lax
from jax.experimental import pallas as pl
from jax.experimental.pallas import tpu as pltpu
from jax.sharding import PartitionSpec as P

SWEEPS = 4
time_step = 0.02
viscosity = 0.05
pressure_shift = 0.25
relaxation = 0.6
coarse_face = 2.0
coarse_reach = 4.0
norm_eps = 1e-06
inner_a = 0.8717401485096066
inner_b = 0.5917001814331423
inner_c = 0.2092992179024789
MESH = pl.DeviceIdType.MESH
DIRS = [(dx, dy) for dx in (-1, 0, 1) for dy in (-1, 0, 1) if (dx, dy) != (0, 0)]


def legendre_seven(points):
    before = points * 0.0 + 1.0
    current = points.copy()
    for degree in range(1, 7):
        following = ((2 * degree + 1) * points * current - degree * before) / (degree + 1)
        before = current
        current = following
    return current


def jacobi_eigen(matrix):
    work = matrix.copy()
    vectors = np.eye(8)
    for sweep_idx in range(10):
        for p_idx in range(7):
            for q_idx in range(p_idx + 1, 8):
                off_value = float(work[p_idx, q_idx])
                if abs(off_value) > 1e-300:
                    theta = 0.5 * math.atan2(
                        2.0 * off_value, float(work[p_idx, p_idx] - work[q_idx, q_idx])
                    )
                    cosine = math.cos(theta)
                    sine = math.sin(theta)
                    rotation = np.eye(8)
                    rotation[p_idx, p_idx] = cosine
                    rotation[q_idx, q_idx] = cosine
                    rotation[q_idx, p_idx] = sine
                    rotation[p_idx, q_idx] = -sine
                    work = rotation.T @ work @ rotation
                    vectors = vectors @ rotation
    eigenvalues = np.array([work[row_idx, row_idx] for row_idx in range(8)])
    return (eigenvalues, vectors)


def gll_tables():
    order = 7
    nodes = np.array([-1.0, -inner_a, -inner_b, -inner_c, inner_c, inner_b, inner_a, 1.0])
    node_values = legendre_seven(nodes)
    weights = 2.0 / (order * (order + 1) * node_values**2)
    derivative = np.zeros((8, 8))
    for row_idx in range(8):
        for col_idx in range(8):
            if row_idx != col_idx:
                derivative[row_idx, col_idx] = node_values[row_idx] / (
                    node_values[col_idx] * (nodes[row_idx] - nodes[col_idx])
                )
    derivative[0, 0] = -order * (order + 1) / 4.0
    derivative[7, 7] = order * (order + 1) / 4.0
    stiffness = derivative.T @ (weights[:, None] * derivative)
    scaling = 1.0 / np.sqrt(weights)
    symmetric = scaling[:, None] * stiffness * scaling[None, :]
    symmetric = 0.5 * (symmetric + symmetric.T)
    eigenvalues, vectors = jacobi_eigen(symmetric)
    modes = scaling[:, None] * vectors
    return (weights, derivative, stiffness, eigenvalues, modes)


def cosine_modes(count):
    row_pos = np.arange(count)[:, None]
    col_pos = np.arange(count)[None, :]
    scaling = np.where(col_pos == 0, math.sqrt(1.0 / count), math.sqrt(2.0 / count))
    basis_cos = scaling * np.cos(math.pi * col_pos * (row_pos + 0.5) / count)
    eigenvalues = 2.0 - 2.0 * np.cos(math.pi * np.arange(count) / count)
    return (basis_cos, eigenvalues)


def halved(table):
    high = table.astype(jnp.bfloat16)
    return high, (table - high.astype(np.float64)).astype(jnp.bfloat16)


def build_tables(count_x, count_y, size_z):
    weights, derivative, stiffness, eigen, modes = gll_tables()
    elem_z = size_z // 8
    lanes = -(-elem_z // 128) * 128
    eye = np.eye(8)
    scaled = stiffness / weights[:, None]
    laplace = np.kron(scaled, eye) + np.kron(eye, scaled)
    left = np.concatenate(
        [
            np.kron(derivative, eye),
            np.kron(eye, derivative),
            viscosity * laplace,
            laplace + pressure_shift * np.eye(64),
            np.kron(modes.T, modes.T),
            np.kron(modes, modes),
        ],
        axis=0,
    )
    blocks = np.eye(16)
    right = np.concatenate(
        [
            np.kron(blocks, matrix).T
            for matrix in (derivative, viscosity * scaled, scaled, modes.T, modes)
        ],
        axis=1,
    )
    weight_xy = np.kron(weights, weights)[:, None]
    weight_3 = weight_xy * np.tile(weights, elem_z)[None, :]
    eigen_xy = (eigen[:, None] + eigen[None, :]).reshape(64, 1)
    inverse = 1.0 / (eigen_xy + np.tile(eigen, elem_z)[None, :] + pressure_shift)
    fields = np.stack([weight_3, inverse])
    modes_y, eig_y = cosine_modes(count_y)
    modes_z, eig_z = cosine_modes(elem_z)
    den = coarse_face * (eig_y[:, None] + eig_z[None, :]) + coarse_reach / float(count_y * count_y)
    down = np.zeros((size_z, lanes))
    down[:, :elem_z] = np.repeat(modes_z, 8, axis=0)
    up = np.zeros((lanes, size_z))
    up[:elem_z] = np.repeat(modes_z, 8, axis=0).T
    green = np.zeros((count_y + 2, count_y, lanes))
    green[1:-1, :, :elem_z] = np.einsum("im,jm,mn->ijn", modes_y, modes_y, 1.0 / den)
    spread = np.repeat(green[1:-1, :, None, :], 8, axis=2)
    spread[:, :, 0] += green[:-2]
    spread[:, :, 7] += green[2:]
    left_hi, left_lo = halved(left)
    right_hi, right_lo = halved(right)
    up_hi, up_lo = halved(up)
    return [
        np.concatenate([left_hi, left_hi, left_lo], axis=1),
        np.concatenate([right_hi, right_hi, right_lo], axis=0),
        np.asarray(fields, np.float32),
        np.concatenate(halved(down), axis=1),
        np.concatenate([up_hi, up_hi, up_lo], axis=0),
        np.asarray(spread, np.float32),
    ]


def split(value):
    high = value.astype(jnp.bfloat16)
    return high, (value - high.astype(jnp.float32)).astype(jnp.bfloat16)


def dot(a, b):
    return jnp.dot(a, b, preferred_element_type=jnp.float32)


def kernel(
    count_x, count_y, size_b, size_z,
    basis_hbm, base_hbm, left_hbm, right_hbm, fields_hbm, down_hbm, up_hbm, spread_hbm,
    out, hess,
    basis, base, left, right, fields, down, up, slopes, spread, field, star, phi, source, state,
    xs, ys, cs, xr, yr, cr,
    coarse_s, coarse_r, red_s, red_r,
    load_sem, fsend, frecv, csend, crecv, rsend, rrecv,
):
    gx = lax.axis_index("gx")
    gy = lax.axis_index("gy")
    total = count_x * count_y
    me = gx * count_y + gy
    tiles = size_z // 128
    width = coarse_s.shape[-1]

    loads = [
        pltpu.make_async_copy(basis_hbm.at[size_b - 1], basis.at[size_b - 1], load_sem.at[0]),
        pltpu.make_async_copy(base_hbm, base, load_sem.at[1]),
        pltpu.make_async_copy(spread_hbm.at[gy], spread, load_sem.at[2]),
        pltpu.make_async_copy(
            basis_hbm.at[pl.ds(0, size_b - 1)], basis.at[pl.ds(0, size_b - 1)], load_sem.at[3]
        ),
        pltpu.make_async_copy(left_hbm, left, load_sem.at[4]),
        pltpu.make_async_copy(right_hbm, right, load_sem.at[5]),
        pltpu.make_async_copy(fields_hbm, fields, load_sem.at[6]),
        pltpu.make_async_copy(down_hbm, down, load_sem.at[7]),
        pltpu.make_async_copy(up_hbm, up, load_sem.at[8]),
    ]
    for pos in (0, 1, 4, 5, 2, 6, 7, 8):
        loads[pos].start()
    barrier = pltpu.get_barrier_semaphore()

    def greet(step, carry):
        other = lax.rem(me + step, total)
        pl.semaphore_signal(
            barrier, inc=1, device_id=(other // count_y, lax.rem(other, count_y)),
            device_id_type=MESH,
        )
        return carry

    lax.fori_loop(1, total, greet, 0)

    def there(dx, dy):
        tests = []
        if dx:
            tests.append((gx > 0) if dx < 0 else (gx < count_x - 1))
        if dy:
            tests.append((gy > 0) if dy < 0 else (gy < count_y - 1))
        return tests[0] if len(tests) == 1 else tests[0] & tests[1]

    def clear(ref):
        ref[...] = jnp.zeros(ref.shape, ref.dtype)

    for dx, dy in DIRS:
        ox, oy = (dx + 1) // 2, (dy + 1) // 2

        @pl.when(jnp.logical_not(there(dx, dy)))
        def _():
            if dy == 0:
                clear(xr.at[:, ox])
                clear(coarse_r.at[:, 2 * ox])
            elif dx == 0:
                clear(yr.at[:, oy])
            else:
                clear(cr.at[:, 2 * ox + oy])

    row = lax.broadcasted_iota(jnp.int32, (64, size_z), 0)
    lane = lax.broadcasted_iota(jnp.int32, (64, size_z), 1)
    upper_z = (lane % 8 == 7) & (lane < size_z - 1)
    lower_z = (lane % 8 == 0) & (lane > 0)

    def halves(test):
        return jnp.where(test, 0.5, 1.0)

    rmult = (
        halves(((row // 8 == 0) & (gx > 0)) | ((row // 8 == 7) & (gx < count_x - 1)))
        * halves(((row % 8 == 0) & (gy > 0)) | ((row % 8 == 7) & (gy < count_y - 1)))
        * halves(upper_z | lower_z)
    )
    weight_3 = fields.at[0]

    def along_z(f):
        after = pltpu.roll(f, size_z - 1, 1)
        before = pltpu.roll(f, 1, 1)
        return f + jnp.where(upper_z, after, 0.0) + jnp.where(lower_z, before, 0.0)

    def by_left(start, stop, f):
        high, low = split(f)
        return dot(left[start:stop, :], jnp.concatenate([high, low, high], axis=0))

    def by_right(start, stop, f):
        stacked = jnp.concatenate([f[:, 128 * t : 128 * t + 128] for t in range(tiles)], axis=0)
        high, low = split(stacked)
        product = dot(
            jnp.concatenate([high, low, high], axis=1), right[:, 128 * start : 128 * stop]
        )
        return [
            jnp.concatenate(
                [product[64 * t : 64 * t + 64, 128 * m : 128 * m + 128] for t in range(tiles)],
                axis=1,
            )
            for m in range(stop - start)
        ]

    def each_copy(round_idx, verb):
        for pos, (dx, dy) in enumerate(DIRS):
            ox, oy = (dx + 1) // 2, (dy + 1) // 2
            if dy == 0:
                src, dst, got = xs.at[round_idx, ox], xr.at[round_idx, 1 - ox], xr.at[round_idx, ox]
            elif dx == 0:
                src, dst, got = ys.at[round_idx, oy], yr.at[round_idx, 1 - oy], yr.at[round_idx, oy]
            else:
                src = cs.at[round_idx, 2 * ox + oy]
                dst = cr.at[round_idx, 2 * (1 - ox) + 1 - oy]
                got = cr.at[round_idx, 2 * ox + oy]

            @pl.when(there(dx, dy))
            def _():
                if verb == "start":
                    pltpu.make_async_remote_copy(
                        src_ref=src, dst_ref=dst,
                        send_sem=fsend.at[round_idx, pos], recv_sem=frecv.at[round_idx, 7 - pos],
                        device_id=(gx + dx, gy + dy), device_id_type=MESH,
                    ).start()
                elif verb == "recv":
                    pltpu.make_async_copy(got, got, frecv.at[round_idx, pos]).wait()
                else:
                    pltpu.make_async_copy(src, src, fsend.at[round_idx, pos]).wait()

    def cut(value):
        return [value[:, 128 * t : 128 * t + 128] for t in range(tiles)]

    def send(value, round_idx, c=0):
        value = along_z(value)
        for t, part in enumerate(cut(value)):
            field[c, t] = part
        xs[round_idx, 0] = value[0:8]
        xs[round_idx, 1] = value[56:64]
        for o in range(2):
            face = jnp.concatenate(
                [field[c, t, pl.ds(7 * o, 8, stride=8), :] for t in range(tiles)], axis=1
            )
            ys[round_idx, o] = face
            cs[round_idx, o] = face[0:1]
            cs[round_idx, 2 + o] = face[7:8]
        each_copy(round_idx, "start")

    def receive(round_idx, c=0):
        each_copy(round_idx, "recv")
        for t in range(tiles):
            lanes = slice(128 * t, 128 * t + 128)
            field[c, t, 0:8, :] += xr[round_idx, 0, :, lanes]
            field[c, t, 56:64, :] += xr[round_idx, 1, :, lanes]
            for o in range(2):
                rows = pl.ds(7 * o, 8, stride=8)
                field[c, t, rows, :] += yr[round_idx, o, :, lanes]
                field[c, t, 7 * o : 7 * o + 1, :] += cr[round_idx, o, :, lanes]
                field[c, t, 56 + 7 * o : 57 + 7 * o, :] += cr[round_idx, 2 + o, :, lanes]
        return jnp.concatenate([field[c, t] for t in range(tiles)], axis=1)

    loads[0].wait()
    pl.semaphore_wait(barrier, total - 1)
    for c in range(3):
        send(basis[size_b - 1, c], c, c)
    loads[3].start()
    for pos in (1, 4, 5):
        loads[pos].wait()
    for c in range(3):
        value = base[c]
        both = by_left(0, 128, value)
        slopes[0, c] = both[:64]
        slopes[1, c] = both[64:]
        slopes[2, c] = by_right(0, 1, value)[0]
    for c in range(3):
        state[c] = receive(c, c) * rmult

    for c in range(3):
        value = state[c]
        products = by_left(0, 192, value)
        along, diffuse = by_right(0, 2, value)
        change = products[128:] + diffuse
        for j, slope in enumerate((products[:64], products[64:128], along)):
            change = change + base[j] * slope + state[j] * slopes[j, c]
        send(change, 3 + c, c)
    for c in range(3):
        star[c] = state[c] - time_step * (receive(3 + c, c) * rmult)

    divergence = (
        by_left(0, 64, star[0]) + by_left(64, 128, star[1]) + by_right(0, 1, star[2])[0]
    )
    source[...] = divergence
    for pos in (2, 6, 7, 8):
        loads[pos].wait()

    def coarse_copies(sweep):
        for pos, dx in enumerate((-1, 0, 1)):
            def to(step, carry, dx=dx, pos=pos):
                copy = pltpu.make_async_remote_copy(
                    src_ref=coarse_s.at[sweep],
                    dst_ref=coarse_r.at[sweep, 2 - pos, gy],
                    send_sem=csend.at[sweep, pos],
                    recv_sem=crecv.at[sweep, 2 - pos],
                    device_id=(gx + dx, lax.rem(gy + step, count_y)),
                    device_id_type=MESH,
                )
                copy.start()
                return carry

            if dx == 0:
                lax.fori_loop(1, count_y, to, 0)
            else:
                @pl.when(there(dx, 0))
                def _():
                    lax.fori_loop(0, count_y, to, 0)

    def coarse_wait(sweep, sems):
        for pos, dx in enumerate((-1, 0, 1)):
            part = coarse_r.at[sweep, pos]
            if dx == 0:
                part = coarse_r.at[sweep, pos, pl.ds(0, count_y - 1)]
            if dx == 0:
                pltpu.make_async_copy(part, part, sems.at[sweep, pos]).wait()
            else:

                @pl.when(there(dx, 0))
                def _():
                    pltpu.make_async_copy(part, part, sems.at[sweep, pos]).wait()

    for sweep in range(SWEEPS):
        if sweep == 0:
            whole = source[...]
        else:
            pressure = phi[...]
            whole = source[...] + by_left(192, 256, pressure) + by_right(2, 3, pressure)[0]
        send(-weight_3[...] * whole, 9 + 2 * sweep)
        resid = receive(9 + 2 * sweep)
        shares = functools.reduce(
            lambda a, b: a + b, [(resid * rmult)[8 * j : 8 * j + 8] for j in range(8)]
        )
        shares = dot(jnp.concatenate(split(shares), axis=0), down[...])
        shares = jnp.sum(
            shares[0:8, :width] + shares[8:16, :width] + shares[0:8, width:],
            axis=0, keepdims=True,
        )
        coarse_s[sweep] = shares
        coarse_copies(sweep)
        coarse_r[sweep, 1, gy] = shares
        local = by_left(256, 320, resid)
        local = by_right(3, 4, local)[0] * fields[1]
        local = by_left(320, 384, local)
        local = by_right(4, 5, local)[0]
        send(local, 10 + 2 * sweep)
        coarse_wait(sweep, crecv)
        parts = []
        for pos in range(3):
            part = spread[0] * coarse_r[sweep, pos, 0]
            for j in range(1, count_y):
                part = part + spread[j] * coarse_r[sweep, pos, j]
            parts.append(part)
        high, low = split(jnp.concatenate(parts, axis=0))
        levels = dot(jnp.concatenate([high, low, high], axis=1), up[...])
        lower, own, upper = levels[0:8], levels[8:16], levels[16:24]
        flat = jnp.concatenate([own + lower] + [own] * 6 + [own + upper], axis=0)
        step_sum = along_z(flat) + receive(10 + 2 * sweep)
        update = relaxation * step_sum * rmult
        phi[...] = update if sweep == 0 else phi[...] + update

    pressure = phi[...]
    both = by_left(0, 128, pressure)
    send(both[:64], 6, 0)
    send(both[64:], 7, 1)
    send(by_right(0, 1, pressure)[0], 8, 2)
    for c in range(3):
        star[c] = star[c] - receive(6 + c, c) * rmult
    loads[3].wait()
    mass = weight_3[...] * rmult * (1.0 / (8.0 * total * (size_z // 8)))
    phi[...] = mass

    def fold(value):
        return functools.reduce(
            lambda a, b: a + b, [value[:, 128 * t : 128 * t + 128] for t in range(tiles)]
        )

    def products_of(step, sums):
        c, x = step // 8, lax.rem(step, 8)
        rows = pl.ds(pl.multiple_of(8 * x, 8), 8)
        weighted = star[c, rows, :] * phi[rows, :]
        return tuple(
            total_k + fold(basis[k, c, rows, :] * weighted) for k, total_k in enumerate(sums)
        )

    zero = jnp.zeros((8, 128), jnp.float32)
    sums = lax.fori_loop(0, 24, products_of, (zero,) * size_b)
    lane_1 = lax.broadcasted_iota(jnp.int32, (1, 128), 1)

    def all_sum(which, value):
        red_s[which] = value

        def to(step, carry):
            other = lax.rem(me + step, total)
            pltpu.make_async_remote_copy(
                src_ref=red_s.at[which], dst_ref=red_r.at[which, me],
                send_sem=rsend.at[which], recv_sem=rrecv.at[which],
                device_id=(other // count_y, lax.rem(other, count_y)), device_id_type=MESH,
            ).start()
            return carry

        lax.fori_loop(1, total, to, 0)
        red_r[which, me] = value
        part = red_r.at[which, pl.ds(0, total - 1)]
        pltpu.make_async_copy(part, part, rrecv.at[which]).wait()
        return functools.reduce(lambda a, b: a + b, [red_r[which, j] for j in range(total)])

    own = jnp.zeros((1, 128), jnp.float32)
    for k in range(size_b):
        value = jnp.sum(jnp.sum(sums[k], axis=0, keepdims=True), axis=1, keepdims=True)
        own = jnp.where(lane_1 == k, value, own)
    hcol = all_sum(0, own)
    spreads = [
        jnp.broadcast_to(
            jnp.sum(jnp.where(lane_1 == k, hcol, 0.0), axis=1, keepdims=True), (8, 128)
        )
        for k in range(size_b)
    ]

    def remainder_of(step, squares):
        c, x = step // 8, lax.rem(step, 8)
        rows = pl.ds(pl.multiple_of(8 * x, 8), 8)
        for t in range(tiles):
            lanes = slice(128 * t, 128 * t + 128)
            value = star[c, rows, lanes]
            for k in range(size_b):
                value = value - spreads[k] * basis[k, c, rows, lanes]
            star[c, rows, lanes] = value
            squares = squares + value * value * phi[rows, lanes]
        return squares

    squares = lax.fori_loop(0, 24, remainder_of, zero)
    squared = jnp.sum(jnp.sum(squares, axis=0, keepdims=True), axis=1, keepdims=True)
    squared = all_sum(1, jnp.broadcast_to(squared, (1, 128)))
    beta = jnp.sqrt(squared + norm_eps)
    hess[...] = jnp.where(lane_1 == size_b, beta, hcol)
    scale = 1.0 / beta[:, 0:1]
    for c in range(3):
        out[c] = star[c] * scale

    for round_idx in range(9 + 2 * SWEEPS):
        each_copy(round_idx, "sent")
    for sweep in range(SWEEPS):
        coarse_wait(sweep, csend)
    for which in range(2):
        part = red_r.at[which, pl.ds(0, total - 1)]
        pltpu.make_async_copy(part, part, rsend.at[which]).wait()


def per_device(basis, base_flow):
    size_b = basis.shape[0]
    components, size_x, size_y, size_z = base_flow.shape
    count_x = lax.axis_size("gx")
    count_y = lax.axis_size("gy")
    tables = build_tables(count_x, count_y, size_z)
    lanes = tables[5].shape[3]
    vmem = functools.partial(pltpu.VMEM, dtype=jnp.float32)
    dma = pltpu.SemaphoreType.DMA
    rounds = 9 + 2 * SWEEPS
    shapes = [(rounds, 2, 8, size_z), (rounds, 2, 8, size_z), (rounds, 4, 1, size_z)]
    exchange = [vmem(shape) for shape in shapes * 2]
    spec_v = pl.BlockSpec(memory_space=pltpu.VMEM)
    spec_any = pl.BlockSpec(memory_space=pl.ANY)
    out, hess = pl.pallas_call(
        functools.partial(kernel, count_x, count_y, size_b, size_z),
        out_shape=(
            jax.ShapeDtypeStruct((3, 64, size_z), jnp.float32),
            jax.ShapeDtypeStruct((1, 128), jnp.float32),
        ),
        in_specs=[spec_any] * 8,
        out_specs=(spec_v, spec_v),
        scratch_shapes=[
            vmem((size_b, 3, 64, size_z)),
            vmem((3, 64, size_z)),
        ]
        + [pltpu.VMEM(table.shape, table.dtype) for table in tables[:5]]
        + [
            vmem((3, 3, 64, size_z)),
            vmem((count_y, 8, lanes)),
            vmem((3, size_z // 128, 64, 128)),
            vmem((3, 64, size_z)),
            vmem((64, size_z)),
            vmem((64, size_z)),
            vmem((3, 64, size_z)),
        ]
        + exchange
        + [
            vmem((SWEEPS, 1, lanes)),
            vmem((SWEEPS, 3, count_y, 1, lanes)),
            vmem((2, 1, 128)),
            vmem((2, count_x * count_y, 1, 128)),
            dma((9,)),
            dma((rounds, 8)),
            dma((rounds, 8)),
            dma((SWEEPS, 3)),
            dma((SWEEPS, 3)),
            dma((2,)),
            dma((2,)),
        ],
        compiler_params=pltpu.CompilerParams(
            collective_id=0, has_side_effects=True, vmem_limit_bytes=60 * 1024 * 1024
        ),
    )(
        basis.reshape(size_b, 3, 64, size_z),
        base_flow.reshape(3, 64, size_z),
        *[jnp.asarray(table) for table in tables],
    )
    return (out.reshape(base_flow.shape), hess[0, : size_b + 1])


def solution(mesh):
    return jax.shard_map(
        per_device,
        mesh=mesh,
        in_specs=(P(None, None, "gx", "gy", None), P(None, "gx", "gy", None)),
        out_specs=(P(None, "gx", "gy", None), P()),
        check_vma=False,
    )
```

```python
import functools
import math

import jax
import jax.numpy as jnp
import numpy as np
from jax import lax
from jax.experimental import pallas as pl
from jax.experimental.pallas import tpu as pltpu
from jax.sharding import PartitionSpec as P

SWEEPS = 4
time_step = 0.02
viscosity = 0.05
pressure_shift = 0.25
relaxation = 0.6
coarse_face = 2.0
coarse_reach = 4.0
norm_eps = 1e-06
inner_a = 0.8717401485096066
inner_b = 0.5917001814331423
inner_c = 0.2092992179024789
MESH = pl.DeviceIdType.MESH
DIRS = [(dx, dy) for dx in (-1, 0, 1) for dy in (-1, 0, 1) if (dx, dy) != (0, 0)]


def legendre_seven(points):
    before = points * 0.0 + 1.0
    current = points.copy()
    for degree in range(1, 7):
        following = ((2 * degree + 1) * points * current - degree * before) / (degree + 1)
        before = current
        current = following
    return current


def jacobi_eigen(matrix):
    work = matrix.copy()
    vectors = np.eye(8)
    for sweep_idx in range(10):
        for p_idx in range(7):
            for q_idx in range(p_idx + 1, 8):
                off_value = float(work[p_idx, q_idx])
                if abs(off_value) > 1e-300:
                    theta = 0.5 * math.atan2(
                        2.0 * off_value, float(work[p_idx, p_idx] - work[q_idx, q_idx])
                    )
                    cosine = math.cos(theta)
                    sine = math.sin(theta)
                    rotation = np.eye(8)
                    rotation[p_idx, p_idx] = cosine
                    rotation[q_idx, q_idx] = cosine
                    rotation[q_idx, p_idx] = sine
                    rotation[p_idx, q_idx] = -sine
                    work = rotation.T @ work @ rotation
                    vectors = vectors @ rotation
    eigenvalues = np.array([work[row_idx, row_idx] for row_idx in range(8)])
    return (eigenvalues, vectors)


def gll_tables():
    order = 7
    nodes = np.array([-1.0, -inner_a, -inner_b, -inner_c, inner_c, inner_b, inner_a, 1.0])
    node_values = legendre_seven(nodes)
    weights = 2.0 / (order * (order + 1) * node_values**2)
    derivative = np.zeros((8, 8))
    for row_idx in range(8):
        for col_idx in range(8):
            if row_idx != col_idx:
                derivative[row_idx, col_idx] = node_values[row_idx] / (
                    node_values[col_idx] * (nodes[row_idx] - nodes[col_idx])
                )
    derivative[0, 0] = -order * (order + 1) / 4.0
    derivative[7, 7] = order * (order + 1) / 4.0
    stiffness = derivative.T @ (weights[:, None] * derivative)
    scaling = 1.0 / np.sqrt(weights)
    symmetric = scaling[:, None] * stiffness * scaling[None, :]
    symmetric = 0.5 * (symmetric + symmetric.T)
    eigenvalues, vectors = jacobi_eigen(symmetric)
    modes = scaling[:, None] * vectors
    return (weights, derivative, stiffness, eigenvalues, modes)


def cosine_modes(count):
    row_pos = np.arange(count)[:, None]
    col_pos = np.arange(count)[None, :]
    scaling = np.where(col_pos == 0, math.sqrt(1.0 / count), math.sqrt(2.0 / count))
    basis_cos = scaling * np.cos(math.pi * col_pos * (row_pos + 0.5) / count)
    eigenvalues = 2.0 - 2.0 * np.cos(math.pi * np.arange(count) / count)
    return (basis_cos, eigenvalues)


def halved(table):
    high = table.astype(jnp.bfloat16)
    return high, (table - high.astype(np.float64)).astype(jnp.bfloat16)


def build_tables(count_x, count_y, size_z):
    weights, derivative, stiffness, eigen, modes = gll_tables()
    elem_z = size_z // 8
    lanes = -(-elem_z // 128) * 128
    eye = np.eye(8)
    scaled = stiffness / weights[:, None]
    laplace = np.kron(scaled, eye) + np.kron(eye, scaled)
    left = np.concatenate(
        [
            np.kron(derivative, eye),
            np.kron(eye, derivative),
            viscosity * laplace,
            laplace + pressure_shift * np.eye(64),
            np.kron(modes.T, modes.T),
            np.kron(modes, modes),
        ],
        axis=0,
    )
    blocks = np.eye(16)
    right = np.concatenate(
        [
            np.kron(blocks, matrix).T
            for matrix in (derivative, viscosity * scaled, scaled, modes.T, modes)
        ],
        axis=1,
    )
    weight_xy = np.kron(weights, weights)[:, None]
    weight_3 = weight_xy * np.tile(weights, elem_z)[None, :]
    eigen_xy = (eigen[:, None] + eigen[None, :]).reshape(64, 1)
    inverse = 1.0 / (eigen_xy + np.tile(eigen, elem_z)[None, :] + pressure_shift)
    fields = np.stack([weight_3, inverse])
    modes_y, eig_y = cosine_modes(count_y)
    modes_z, eig_z = cosine_modes(elem_z)
    den = coarse_face * (eig_y[:, None] + eig_z[None, :]) + coarse_reach / float(count_y * count_y)
    down = np.zeros((size_z, lanes))
    down[:, :elem_z] = np.repeat(modes_z, 8, axis=0)
    up = np.zeros((lanes, size_z))
    up[:elem_z] = np.repeat(modes_z, 8, axis=0).T
    green = np.zeros((count_y + 2, count_y, lanes))
    green[1:-1, :, :elem_z] = np.einsum("im,jm,mn->ijn", modes_y, modes_y, 1.0 / den)
    spread = np.repeat(green[1:-1, :, None, :], 8, axis=2)
    spread[:, :, 0] += green[:-2]
    spread[:, :, 7] += green[2:]
    left_hi, left_lo = halved(left)
    right_hi, right_lo = halved(right)
    up_hi, up_lo = halved(up)
    return [
        np.concatenate([left_hi, left_hi, left_lo], axis=1),
        np.concatenate([right_hi, right_hi, right_lo], axis=0),
        np.asarray(fields, np.float32),
        np.concatenate(halved(down), axis=1),
        np.concatenate([up_hi, up_hi, up_lo], axis=0),
        np.asarray(spread, np.float32),
    ]


def split(value):
    high = value.astype(jnp.bfloat16)
    return high, (value - high.astype(jnp.float32)).astype(jnp.bfloat16)


def dot(a, b):
    return jnp.dot(a, b, preferred_element_type=jnp.float32)


def kernel(
    count_x, count_y, size_b, size_z,
    basis_hbm, base_hbm, left_hbm, right_hbm, fields_hbm, down_hbm, up_hbm, spread_hbm,
    out, hess, norm,
    basis, base, left, right, fields, down, up, slopes, spread, field, star, phi, source, state,
    xs3, ys3, cs3, xr3, yr3, cr3,
    xs1, ys1, cs1, xr1, yr1, cr1,
    coarse_s, coarse_r, red_s, red_r,
    load_sem, send3, recv3, send1, recv1, csend, crecv, rsend, rrecv,
):
    gx = lax.axis_index("gx")
    gy = lax.axis_index("gy")
    total = count_x * count_y
    me = gx * count_y + gy
    tiles = size_z // 128
    width = coarse_s.shape[-1]

    loads = [
        pltpu.make_async_copy(basis_hbm.at[size_b - 1], basis.at[size_b - 1], load_sem.at[0]),
        pltpu.make_async_copy(base_hbm, base, load_sem.at[1]),
        pltpu.make_async_copy(spread_hbm.at[gy], spread, load_sem.at[2]),
        pltpu.make_async_copy(
            basis_hbm.at[pl.ds(0, size_b - 1)], basis.at[pl.ds(0, size_b - 1)], load_sem.at[3]
        ),
        pltpu.make_async_copy(left_hbm, left, load_sem.at[4]),
        pltpu.make_async_copy(right_hbm, right, load_sem.at[5]),
        pltpu.make_async_copy(fields_hbm, fields, load_sem.at[6]),
        pltpu.make_async_copy(down_hbm, down, load_sem.at[7]),
        pltpu.make_async_copy(up_hbm, up, load_sem.at[8]),
    ]
    for pos in (0, 1, 4, 5, 2, 6, 7, 8):
        loads[pos].start()
    barrier = pltpu.get_barrier_semaphore()

    def greet(step, carry):
        other = lax.rem(me + step, total)
        pl.semaphore_signal(
            barrier, inc=1, device_id=(other // count_y, lax.rem(other, count_y)),
            device_id_type=MESH,
        )
        return carry

    lax.fori_loop(1, total, greet, 0)

    def there(dx, dy):
        tests = []
        if dx:
            tests.append((gx > 0) if dx < 0 else (gx < count_x - 1))
        if dy:
            tests.append((gy > 0) if dy < 0 else (gy < count_y - 1))
        return tests[0] if len(tests) == 1 else tests[0] & tests[1]

    def clear(ref):
        ref[...] = jnp.zeros(ref.shape, ref.dtype)

    for dx, dy in DIRS:
        ox, oy = (dx + 1) // 2, (dy + 1) // 2

        @pl.when(jnp.logical_not(there(dx, dy)))
        def _():
            for xr, yr, cr in ((xr3, yr3, cr3), (xr1, yr1, cr1)):
                if dy == 0:
                    clear(xr.at[:, ox])
                elif dx == 0:
                    clear(yr.at[:, oy])
                else:
                    clear(cr.at[:, 2 * ox + oy])
            if dy == 0:
                clear(coarse_r.at[:, 2 * ox])

    row = lax.broadcasted_iota(jnp.int32, (64, size_z), 0)
    lane = lax.broadcasted_iota(jnp.int32, (64, size_z), 1)
    upper_z = (lane % 8 == 7) & (lane < size_z - 1)
    lower_z = (lane % 8 == 0) & (lane > 0)

    def halves(test):
        return jnp.where(test, 0.5, 1.0)

    rmult = (
        halves(((row // 8 == 0) & (gx > 0)) | ((row // 8 == 7) & (gx < count_x - 1)))
        * halves(((row % 8 == 0) & (gy > 0)) | ((row % 8 == 7) & (gy < count_y - 1)))
        * halves(upper_z | lower_z)
    )
    weight_3 = fields.at[0]

    def along_z(f):
        after = pltpu.roll(f, size_z - 1, 1)
        before = pltpu.roll(f, 1, 1)
        return f + jnp.where(upper_z, after, 0.0) + jnp.where(lower_z, before, 0.0)

    def by_left(start, stop, f):
        high, low = split(f)
        return dot(left[start:stop, :], jnp.concatenate([high, low, high], axis=0))

    def by_right(start, stop, f):
        stacked = jnp.concatenate([f[:, 128 * t : 128 * t + 128] for t in range(tiles)], axis=0)
        high, low = split(stacked)
        product = dot(
            jnp.concatenate([high, low, high], axis=1), right[:, 128 * start : 128 * stop]
        )
        return [
            jnp.concatenate(
                [product[64 * t : 64 * t + 64, 128 * m : 128 * m + 128] for t in range(tiles)],
                axis=1,
            )
            for m in range(stop - start)
        ]

    def buffers(wide):
        if wide:
            return (xs3, ys3, cs3, xr3, yr3, cr3, send3, recv3)
        return (xs1, ys1, cs1, xr1, yr1, cr1, send1, recv1)

    def each_copy(round_idx, wide, verb):
        xs, ys, cs, xr, yr, cr, ss, rs = buffers(wide)
        for pos, (dx, dy) in enumerate(DIRS):
            ox, oy = (dx + 1) // 2, (dy + 1) // 2
            if dy == 0:
                src, dst, got = xs.at[round_idx, ox], xr.at[round_idx, 1 - ox], xr.at[round_idx, ox]
            elif dx == 0:
                src, dst, got = ys.at[round_idx, oy], yr.at[round_idx, 1 - oy], yr.at[round_idx, oy]
            else:
                src = cs.at[round_idx, 2 * ox + oy]
                dst = cr.at[round_idx, 2 * (1 - ox) + 1 - oy]
                got = cr.at[round_idx, 2 * ox + oy]

            @pl.when(there(dx, dy))
            def _():
                if verb == "start":
                    pltpu.make_async_remote_copy(
                        src_ref=src, dst_ref=dst,
                        send_sem=ss.at[round_idx, pos], recv_sem=rs.at[round_idx, 7 - pos],
                        device_id=(gx + dx, gy + dy), device_id_type=MESH,
                    ).start()
                elif verb == "recv":
                    pltpu.make_async_copy(got, got, rs.at[round_idx, pos]).wait()
                else:
                    pltpu.make_async_copy(src, src, ss.at[round_idx, pos]).wait()

    def cut(value):
        return [value[:, 128 * t : 128 * t + 128] for t in range(tiles)]

    def send(values, round_idx, wide):
        xs, ys, cs = buffers(wide)[:3]
        for c, value in enumerate(values):
            value = along_z(value)
            for t, part in enumerate(cut(value)):
                field[c, t] = part
            xs[round_idx, 0, c] = value[0:8]
            xs[round_idx, 1, c] = value[56:64]
            for o in range(2):
                face = jnp.concatenate(
                    [field[c, t, pl.ds(7 * o, 8, stride=8), :] for t in range(tiles)], axis=1
                )
                ys[round_idx, o, c] = face
                cs[round_idx, o, c] = face[0:1]
                cs[round_idx, 2 + o, c] = face[7:8]
        each_copy(round_idx, wide, "start")

    def receive(count, round_idx, wide):
        xr, yr, cr = buffers(wide)[3:6]
        each_copy(round_idx, wide, "recv")
        results = []
        for c in range(count):
            for t in range(tiles):
                lanes = slice(128 * t, 128 * t + 128)
                field[c, t, 0:8, :] += xr[round_idx, 0, c, :, lanes]
                field[c, t, 56:64, :] += xr[round_idx, 1, c, :, lanes]
                for o in range(2):
                    rows = pl.ds(7 * o, 8, stride=8)
                    field[c, t, rows, :] += yr[round_idx, o, c, :, lanes]
                    field[c, t, 7 * o : 7 * o + 1, :] += cr[round_idx, o, c, :, lanes]
                    field[c, t, 56 + 7 * o : 57 + 7 * o, :] += cr[round_idx, 2 + o, c, :, lanes]
            results.append(jnp.concatenate([field[c, t] for t in range(tiles)], axis=1))
        return results

    loads[0].wait()
    first = [basis[size_b - 1, c] for c in range(3)]
    pl.semaphore_wait(barrier, total - 1)
    send(first, 0, True)
    loads[3].start()
    for pos in (1, 4, 5):
        loads[pos].wait()
    for c in range(3):
        value = base[c]
        both = by_left(0, 128, value)
        slopes[0, c] = both[:64]
        slopes[1, c] = both[64:]
        slopes[2, c] = by_right(0, 1, value)[0]
    for c, value in enumerate(receive(3, 0, True)):
        state[c] = value * rmult

    sums = []
    for c in range(3):
        value = state[c]
        products = by_left(0, 192, value)
        along, diffuse = by_right(0, 2, value)
        change = products[128:] + diffuse
        for j, slope in enumerate((products[:64], products[64:128], along)):
            change = change + base[j] * slope + state[j] * slopes[j, c]
        sums.append(change)
    send(sums, 1, True)
    for c, value in enumerate(receive(3, 1, True)):
        star[c] = state[c] - time_step * (value * rmult)

    divergence = (
        by_left(0, 64, star[0]) + by_left(64, 128, star[1]) + by_right(0, 1, star[2])[0]
    )
    source[...] = divergence
    for pos in (2, 6, 7, 8):
        loads[pos].wait()

    def coarse_copies(sweep):
        for pos, dx in enumerate((-1, 0, 1)):
            def to(step, carry, dx=dx, pos=pos):
                copy = pltpu.make_async_remote_copy(
                    src_ref=coarse_s.at[sweep],
                    dst_ref=coarse_r.at[sweep, 2 - pos, gy],
                    send_sem=csend.at[sweep, pos],
                    recv_sem=crecv.at[sweep, 2 - pos],
                    device_id=(gx + dx, lax.rem(gy + step, count_y)),
                    device_id_type=MESH,
                )
                copy.start()
                return carry

            if dx == 0:
                lax.fori_loop(1, count_y, to, 0)
            else:
                @pl.when(there(dx, 0))
                def _():
                    lax.fori_loop(0, count_y, to, 0)

    def coarse_wait(sweep, sems):
        for pos, dx in enumerate((-1, 0, 1)):
            part = coarse_r.at[sweep, pos]
            if dx == 0:
                part = coarse_r.at[sweep, pos, pl.ds(0, count_y - 1)]
            if dx == 0:
                pltpu.make_async_copy(part, part, sems.at[sweep, pos]).wait()
            else:

                @pl.when(there(dx, 0))
                def _():
                    pltpu.make_async_copy(part, part, sems.at[sweep, pos]).wait()

    for sweep in range(SWEEPS):
        if sweep == 0:
            whole = source[...]
        else:
            pressure = phi[...]
            whole = source[...] + by_left(192, 256, pressure) + by_right(2, 3, pressure)[0]
        send([-weight_3[...] * whole], 2 * sweep, False)
        resid = receive(1, 2 * sweep, False)[0]
        shares = functools.reduce(
            lambda a, b: a + b, [(resid * rmult)[8 * j : 8 * j + 8] for j in range(8)]
        )
        shares = dot(jnp.concatenate(split(shares), axis=0), down[...])
        shares = jnp.sum(
            shares[0:8, :width] + shares[8:16, :width] + shares[0:8, width:],
            axis=0, keepdims=True,
        )
        coarse_s[sweep] = shares
        coarse_copies(sweep)
        coarse_r[sweep, 1, gy] = shares
        local = by_left(256, 320, resid)
        local = by_right(3, 4, local)[0] * fields[1]
        local = by_left(320, 384, local)
        local = by_right(4, 5, local)[0]
        send([local], 2 * sweep + 1, False)
        coarse_wait(sweep, crecv)
        parts = []
        for pos in range(3):
            part = spread[0] * coarse_r[sweep, pos, 0]
            for j in range(1, count_y):
                part = part + spread[j] * coarse_r[sweep, pos, j]
            parts.append(part)
        high, low = split(jnp.concatenate(parts, axis=0))
        levels = dot(jnp.concatenate([high, low, high], axis=1), up[...])
        lower, own, upper = levels[0:8], levels[8:16], levels[16:24]
        flat = jnp.concatenate([own + lower] + [own] * 6 + [own + upper], axis=0)
        step_sum = along_z(flat) + receive(1, 2 * sweep + 1, False)[0]
        update = relaxation * step_sum * rmult
        phi[...] = update if sweep == 0 else phi[...] + update

    pressure = phi[...]
    both = by_left(0, 128, pressure)
    send([both[:64], both[64:], by_right(0, 1, pressure)[0]], 2, True)
    source[...] = weight_3[...] * rmult * (1.0 / (8.0 * total * (size_z // 8)))
    loads[3].wait()
    for c, value in enumerate(receive(3, 2, True)):
        star[c] = star[c] - value * rmult

    def fold(value):
        return functools.reduce(
            lambda a, b: a + b, [value[:, 128 * t : 128 * t + 128] for t in range(tiles)]
        )

    def products_of(step, sums):
        c, x = step // 8, lax.rem(step, 8)
        rows = pl.ds(pl.multiple_of(8 * x, 8), 8)
        weighted = star[c, rows, :] * source[rows, :]
        return tuple(
            total_k + fold(basis[k, c, rows, :] * weighted) for k, total_k in enumerate(sums)
        )

    zero = jnp.zeros((8, 128), jnp.float32)
    sums = lax.fori_loop(0, 24, products_of, (zero,) * size_b)
    lane_1 = lax.broadcasted_iota(jnp.int32, (1, 128), 1)

    def all_sum(which, value):
        red_s[which] = value

        def to(step, carry):
            other = lax.rem(me + step, total)
            pltpu.make_async_remote_copy(
                src_ref=red_s.at[which], dst_ref=red_r.at[which, me],
                send_sem=rsend.at[which], recv_sem=rrecv.at[which],
                device_id=(other // count_y, lax.rem(other, count_y)), device_id_type=MESH,
            ).start()
            return carry

        lax.fori_loop(1, total, to, 0)
        red_r[which, me] = value
        if which == 0:
            for round_idx in range(2 * SWEEPS):
                each_copy(round_idx, False, "sent")
        else:
            for round_idx in range(3):
                each_copy(round_idx, True, "sent")
            for sweep in range(SWEEPS):
                coarse_wait(sweep, csend)
        part = red_r.at[which, pl.ds(0, total - 1)]
        pltpu.make_async_copy(part, part, rrecv.at[which]).wait()
        pltpu.make_async_copy(part, part, rsend.at[which]).wait()
        return functools.reduce(lambda a, b: a + b, [red_r[which, j] for j in range(total)])

    own = jnp.zeros((1, 128), jnp.float32)
    for k in range(size_b):
        value = jnp.sum(jnp.sum(sums[k], axis=0, keepdims=True), axis=1, keepdims=True)
        own = jnp.where(lane_1 == k, value, own)
    hcol = all_sum(0, own)
    spreads = [
        jnp.broadcast_to(
            jnp.sum(jnp.where(lane_1 == k, hcol, 0.0), axis=1, keepdims=True), (8, 128)
        )
        for k in range(size_b)
    ]

    def remainder_of(step, squares):
        c, x = step // 8, lax.rem(step, 8)
        rows = pl.ds(pl.multiple_of(8 * x, 8), 8)
        for t in range(tiles):
            lanes = slice(128 * t, 128 * t + 128)
            value = star[c, rows, lanes]
            for k in range(size_b):
                value = value - spreads[k] * basis[k, c, rows, lanes]
            star[c, rows, lanes] = value
            squares = squares + value * value * source[rows, lanes]
        return squares

    squares = lax.fori_loop(0, 24, remainder_of, zero)
    store = pltpu.make_async_copy(star, out, load_sem.at[9])
    store.start()
    squared = jnp.sum(jnp.sum(squares, axis=0, keepdims=True), axis=1, keepdims=True)
    squared = all_sum(1, jnp.broadcast_to(squared, (1, 128)))
    beta = jnp.sqrt(squared + norm_eps)
    hess[...] = jnp.where(lane_1 == size_b, beta, hcol)
    norm[...] = jnp.broadcast_to(beta[:, 0:1], norm.shape)
    store.wait()


def per_device(basis, base_flow):
    size_b = basis.shape[0]
    components, size_x, size_y, size_z = base_flow.shape
    count_x = lax.axis_size("gx")
    count_y = lax.axis_size("gy")
    tables = build_tables(count_x, count_y, size_z)
    lanes = tables[5].shape[3]
    vmem = functools.partial(pltpu.VMEM, dtype=jnp.float32)
    dma = pltpu.SemaphoreType.DMA
    exchange = []
    for rounds, comps in ((3, 3), (2 * SWEEPS, 1)):
        shapes = [
            (rounds, 2, comps, 8, size_z),
            (rounds, 2, comps, 8, size_z),
            (rounds, 4, comps, 1, size_z),
        ]
        exchange += [vmem(shape) for shape in shapes * 2]
    spec_v = pl.BlockSpec(memory_space=pltpu.VMEM)
    spec_any = pl.BlockSpec(memory_space=pl.ANY)
    out, hess, norm = pl.pallas_call(
        functools.partial(kernel, count_x, count_y, size_b, size_z),
        out_shape=(
            jax.ShapeDtypeStruct((3, 64, size_z), jnp.float32),
            jax.ShapeDtypeStruct((1, 128), jnp.float32),
            jax.ShapeDtypeStruct((1, size_z), jnp.float32),
        ),
        in_specs=[spec_any] * 8,
        out_specs=(spec_any, spec_v, spec_v),
        scratch_shapes=[
            vmem((size_b, 3, 64, size_z)),
            vmem((3, 64, size_z)),
        ]
        + [pltpu.VMEM(table.shape, table.dtype) for table in tables[:5]]
        + [
            vmem((3, 3, 64, size_z)),
            vmem((count_y, 8, lanes)),
            vmem((3, size_z // 128, 64, 128)),
            vmem((3, 64, size_z)),
            vmem((64, size_z)),
            vmem((64, size_z)),
            vmem((3, 64, size_z)),
        ]
        + exchange
        + [
            vmem((SWEEPS, 1, lanes)),
            vmem((SWEEPS, 3, count_y, 1, lanes)),
            vmem((2, 1, 128)),
            vmem((2, count_x * count_y, 1, 128)),
            dma((10,)),
            dma((3, 8)),
            dma((3, 8)),
            dma((2 * SWEEPS, 8)),
            dma((2 * SWEEPS, 8)),
            dma((SWEEPS, 3)),
            dma((SWEEPS, 3)),
            dma((2,)),
            dma((2,)),
        ],
        compiler_params=pltpu.CompilerParams(
            collective_id=0, has_side_effects=True, vmem_limit_bytes=60 * 1024 * 1024
        ),
    )(
        basis.reshape(size_b, 3, 64, size_z),
        base_flow.reshape(3, 64, size_z),
        *[jnp.asarray(table) for table in tables],
    )
    return (out.reshape(base_flow.shape) / norm[0], hess[0, : size_b + 1])


def solution(mesh):
    return jax.shard_map(
        per_device,
        mesh=mesh,
        in_specs=(P(None, None, "gx", "gy", None), P(None, "gx", "gy", None)),
        out_specs=(P(None, "gx", "gy", None), P()),
        check_vma=False,
    )
```

```python
import functools
import math

import jax
import jax.numpy as jnp
import numpy as np
from jax import lax
from jax.experimental import pallas as pl
from jax.experimental.pallas import tpu as pltpu
from jax.sharding import PartitionSpec as P

SWEEPS = 4
time_step = 0.02
viscosity = 0.05
pressure_shift = 0.25
relaxation = 0.6
coarse_face = 2.0
coarse_reach = 4.0
norm_eps = 1e-06
inner_a = 0.8717401485096066
inner_b = 0.5917001814331423
inner_c = 0.2092992179024789
MESH = pl.DeviceIdType.MESH
DIRS = [(dx, dy) for dx in (-1, 0, 1) for dy in (-1, 0, 1) if (dx, dy) != (0, 0)]


def legendre_seven(points):
    before = points * 0.0 + 1.0
    current = points.copy()
    for degree in range(1, 7):
        following = ((2 * degree + 1) * points * current - degree * before) / (degree + 1)
        before = current
        current = following
    return current


def jacobi_eigen(matrix):
    work = matrix.copy()
    vectors = np.eye(8)
    for sweep_idx in range(10):
        for p_idx in range(7):
            for q_idx in range(p_idx + 1, 8):
                off_value = float(work[p_idx, q_idx])
                if abs(off_value) > 1e-300:
                    theta = 0.5 * math.atan2(
                        2.0 * off_value, float(work[p_idx, p_idx] - work[q_idx, q_idx])
                    )
                    cosine = math.cos(theta)
                    sine = math.sin(theta)
                    rotation = np.eye(8)
                    rotation[p_idx, p_idx] = cosine
                    rotation[q_idx, q_idx] = cosine
                    rotation[q_idx, p_idx] = sine
                    rotation[p_idx, q_idx] = -sine
                    work = rotation.T @ work @ rotation
                    vectors = vectors @ rotation
    eigenvalues = np.array([work[row_idx, row_idx] for row_idx in range(8)])
    return (eigenvalues, vectors)


def gll_tables():
    order = 7
    nodes = np.array([-1.0, -inner_a, -inner_b, -inner_c, inner_c, inner_b, inner_a, 1.0])
    node_values = legendre_seven(nodes)
    weights = 2.0 / (order * (order + 1) * node_values**2)
    derivative = np.zeros((8, 8))
    for row_idx in range(8):
        for col_idx in range(8):
            if row_idx != col_idx:
                derivative[row_idx, col_idx] = node_values[row_idx] / (
                    node_values[col_idx] * (nodes[row_idx] - nodes[col_idx])
                )
    derivative[0, 0] = -order * (order + 1) / 4.0
    derivative[7, 7] = order * (order + 1) / 4.0
    stiffness = derivative.T @ (weights[:, None] * derivative)
    scaling = 1.0 / np.sqrt(weights)
    symmetric = scaling[:, None] * stiffness * scaling[None, :]
    symmetric = 0.5 * (symmetric + symmetric.T)
    eigenvalues, vectors = jacobi_eigen(symmetric)
    modes = scaling[:, None] * vectors
    return (weights, derivative, stiffness, eigenvalues, modes)


def cosine_modes(count):
    row_pos = np.arange(count)[:, None]
    col_pos = np.arange(count)[None, :]
    scaling = np.where(col_pos == 0, math.sqrt(1.0 / count), math.sqrt(2.0 / count))
    basis_cos = scaling * np.cos(math.pi * col_pos * (row_pos + 0.5) / count)
    eigenvalues = 2.0 - 2.0 * np.cos(math.pi * np.arange(count) / count)
    return (basis_cos, eigenvalues)


def halved(table):
    high = table.astype(jnp.bfloat16)
    return high, (table - high.astype(np.float64)).astype(jnp.bfloat16)


def build_tables(count_x, count_y, size_z):
    weights, derivative, stiffness, eigen, modes = gll_tables()
    elem_z = size_z // 8
    lanes = -(-elem_z // 128) * 128
    eye = np.eye(8)
    scaled = stiffness / weights[:, None]
    laplace = np.kron(scaled, eye) + np.kron(eye, scaled)
    left = np.concatenate(
        [
            np.kron(derivative, eye),
            np.kron(eye, derivative),
            viscosity * laplace,
            laplace + pressure_shift * np.eye(64),
            np.kron(modes.T, modes.T),
            np.kron(modes, modes),
        ],
        axis=0,
    )
    blocks = np.eye(16)
    right = np.concatenate(
        [
            np.kron(blocks, matrix).T
            for matrix in (derivative, viscosity * scaled, scaled, modes.T, modes)
        ],
        axis=1,
    )
    weight_xy = np.kron(weights, weights)[:, None]
    weight_3 = weight_xy * np.tile(weights, elem_z)[None, :]
    eigen_xy = (eigen[:, None] + eigen[None, :]).reshape(64, 1)
    inverse = 1.0 / (eigen_xy + np.tile(eigen, elem_z)[None, :] + pressure_shift)
    fields = np.stack([weight_3, inverse])
    modes_y, eig_y = cosine_modes(count_y)
    modes_z, eig_z = cosine_modes(elem_z)
    den = coarse_face * (eig_y[:, None] + eig_z[None, :]) + coarse_reach / float(count_y * count_y)
    down = np.zeros((size_z, lanes))
    down[:, :elem_z] = np.repeat(modes_z, 8, axis=0)
    up = np.zeros((lanes, size_z))
    up[:elem_z] = np.repeat(modes_z, 8, axis=0).T
    green = np.zeros((count_y + 2, count_y, lanes))
    green[1:-1, :, :elem_z] = np.einsum("im,jm,mn->ijn", modes_y, modes_y, 1.0 / den)
    spread = np.repeat(green[1:-1, :, None, :], 8, axis=2)
    spread[:, :, 0] += green[:-2]
    spread[:, :, 7] += green[2:]
    left_hi, left_lo = halved(left)
    right_hi, right_lo = halved(right)
    up_hi, up_lo = halved(up)
    return [
        np.concatenate([left_hi, left_hi, left_lo], axis=1),
        np.concatenate([right_hi, right_hi, right_lo], axis=0),
        np.asarray(fields, np.float32),
        np.concatenate(halved(down), axis=1),
        np.concatenate([up_hi, up_hi, up_lo], axis=0),
        np.asarray(spread, np.float32),
    ]


def split(value):
    high = value.astype(jnp.bfloat16)
    return high, (value - high.astype(jnp.float32)).astype(jnp.bfloat16)


def dot(a, b):
    return jnp.dot(a, b, preferred_element_type=jnp.float32)


def kernel(
    count_x, count_y, size_b, size_z,
    basis_hbm, base_hbm, left_hbm, right_hbm, fields_hbm, down_hbm, up_hbm, spread_hbm,
    out, hess, norm,
    basis, base, left, right, fields, down, up, slopes, spread, field, star, phi, source, state,
    xs3, ys3, cs3, xr3, yr3, cr3,
    xs1, ys1, cs1, xr1, yr1, cr1,
    coarse_s, coarse_r, red_s, red_r,
    load_sem, send3, recv3, send1, recv1, csend, crecv, rsend, rrecv,
):
    gx = lax.axis_index("gx")
    gy = lax.axis_index("gy")
    total = count_x * count_y
    me = gx * count_y + gy
    tiles = size_z // 128
    width = coarse_s.shape[-1]

    loads = [
        pltpu.make_async_copy(basis_hbm.at[size_b - 1], basis.at[size_b - 1], load_sem.at[0]),
        pltpu.make_async_copy(base_hbm, base, load_sem.at[1]),
        pltpu.make_async_copy(spread_hbm.at[gy], spread, load_sem.at[2]),
        pltpu.make_async_copy(
            basis_hbm.at[pl.ds(0, size_b - 1)], basis.at[pl.ds(0, size_b - 1)], load_sem.at[3]
        ),
        pltpu.make_async_copy(left_hbm, left, load_sem.at[4]),
        pltpu.make_async_copy(right_hbm, right, load_sem.at[5]),
        pltpu.make_async_copy(fields_hbm, fields, load_sem.at[6]),
        pltpu.make_async_copy(down_hbm, down, load_sem.at[7]),
        pltpu.make_async_copy(up_hbm, up, load_sem.at[8]),
    ]
    for pos in (0, 1, 4, 5, 2, 6, 7, 8):
        loads[pos].start()
    barrier = pltpu.get_barrier_semaphore()

    def greet(step, carry):
        other = lax.rem(me + step, total)
        pl.semaphore_signal(
            barrier, inc=1, device_id=(other // count_y, lax.rem(other, count_y)),
            device_id_type=MESH,
        )
        return carry

    lax.fori_loop(1, total, greet, 0)

    def there(dx, dy):
        tests = []
        if dx:
            tests.append((gx > 0) if dx < 0 else (gx < count_x - 1))
        if dy:
            tests.append((gy > 0) if dy < 0 else (gy < count_y - 1))
        return tests[0] if len(tests) == 1 else tests[0] & tests[1]

    def clear(ref):
        ref[...] = jnp.zeros(ref.shape, ref.dtype)

    for dx, dy in DIRS:
        ox, oy = (dx + 1) // 2, (dy + 1) // 2

        @pl.when(jnp.logical_not(there(dx, dy)))
        def _():
            for xr, yr, cr in ((xr3, yr3, cr3), (xr1, yr1, cr1)):
                if dy == 0:
                    clear(xr.at[:, ox])
                elif dx == 0:
                    clear(yr.at[:, oy])
                else:
                    clear(cr.at[:, 2 * ox + oy])
            if dy == 0:
                clear(coarse_r.at[:, 2 * ox])

    row = lax.broadcasted_iota(jnp.int32, (64, size_z), 0)
    lane = lax.broadcasted_iota(jnp.int32, (64, size_z), 1)
    upper_z = (lane % 8 == 7) & (lane < size_z - 1)
    lower_z = (lane % 8 == 0) & (lane > 0)

    def halves(test):
        return jnp.where(test, 0.5, 1.0)

    rmult = (
        halves(((row // 8 == 0) & (gx > 0)) | ((row // 8 == 7) & (gx < count_x - 1)))
        * halves(((row % 8 == 0) & (gy > 0)) | ((row % 8 == 7) & (gy < count_y - 1)))
        * halves(upper_z | lower_z)
    )
    weight_3 = fields.at[0]

    def along_z(f):
        after = pltpu.roll(f, size_z - 1, 1)
        before = pltpu.roll(f, 1, 1)
        return f + jnp.where(upper_z, after, 0.0) + jnp.where(lower_z, before, 0.0)

    def by_left(start, stop, f):
        high, low = split(f)
        return dot(left[start:stop, :], jnp.concatenate([high, low, high], axis=0))

    def by_right(start, stop, f):
        stacked = jnp.concatenate([f[:, 128 * t : 128 * t + 128] for t in range(tiles)], axis=0)
        high, low = split(stacked)
        product = dot(
            jnp.concatenate([high, low, high], axis=1), right[:, 128 * start : 128 * stop]
        )
        return [
            jnp.concatenate(
                [product[64 * t : 64 * t + 64, 128 * m : 128 * m + 128] for t in range(tiles)],
                axis=1,
            )
            for m in range(stop - start)
        ]

    def buffers(wide):
        if wide:
            return (xs3, ys3, cs3, xr3, yr3, cr3, send3, recv3)
        return (xs1, ys1, cs1, xr1, yr1, cr1, send1, recv1)

    def each_copy(round_idx, wide, verb):
        xs, ys, cs, xr, yr, cr, ss, rs = buffers(wide)
        for pos, (dx, dy) in enumerate(DIRS):
            ox, oy = (dx + 1) // 2, (dy + 1) // 2
            if dy == 0:
                src, dst, got = xs.at[round_idx, ox], xr.at[round_idx, 1 - ox], xr.at[round_idx, ox]
            elif dx == 0:
                src, dst, got = ys.at[round_idx, oy], yr.at[round_idx, 1 - oy], yr.at[round_idx, oy]
            else:
                src = cs.at[round_idx, 2 * ox + oy]
                dst = cr.at[round_idx, 2 * (1 - ox) + 1 - oy]
                got = cr.at[round_idx, 2 * ox + oy]

            @pl.when(there(dx, dy))
            def _():
                if verb == "start":
                    pltpu.make_async_remote_copy(
                        src_ref=src, dst_ref=dst,
                        send_sem=ss.at[round_idx, pos], recv_sem=rs.at[round_idx, 7 - pos],
                        device_id=(gx + dx, gy + dy), device_id_type=MESH,
                    ).start()
                elif verb == "recv":
                    pltpu.make_async_copy(got, got, rs.at[round_idx, pos]).wait()
                else:
                    pltpu.make_async_copy(src, src, ss.at[round_idx, pos]).wait()

    def cut(value):
        return [value[:, 128 * t : 128 * t + 128] for t in range(tiles)]

    def send(values, round_idx, wide):
        xs, ys, cs = buffers(wide)[:3]
        for c, value in enumerate(values):
            value = along_z(value)
            for t, part in enumerate(cut(value)):
                field[c, t] = part
            xs[round_idx, 0, c] = value[0:8]
            xs[round_idx, 1, c] = value[56:64]
            for o in range(2):
                face = jnp.concatenate(
                    [field[c, t, pl.ds(7 * o, 8, stride=8), :] for t in range(tiles)], axis=1
                )
                ys[round_idx, o, c] = face
                cs[round_idx, o, c] = face[0:1]
                cs[round_idx, 2 + o, c] = face[7:8]
        each_copy(round_idx, wide, "start")

    def receive(count, round_idx, wide):
        xr, yr, cr = buffers(wide)[3:6]
        each_copy(round_idx, wide, "recv")
        results = []
        for c in range(count):
            for t in range(tiles):
                lanes = slice(128 * t, 128 * t + 128)
                field[c, t, 0:8, :] += xr[round_idx, 0, c, :, lanes]
                field[c, t, 56:64, :] += xr[round_idx, 1, c, :, lanes]
                for o in range(2):
                    rows = pl.ds(7 * o, 8, stride=8)
                    field[c, t, rows, :] += yr[round_idx, o, c, :, lanes]
                    field[c, t, 7 * o : 7 * o + 1, :] += cr[round_idx, o, c, :, lanes]
                    field[c, t, 56 + 7 * o : 57 + 7 * o, :] += cr[round_idx, 2 + o, c, :, lanes]
            results.append(jnp.concatenate([field[c, t] for t in range(tiles)], axis=1))
        return results

    loads[0].wait()
    first = [basis[size_b - 1, c] for c in range(3)]
    pl.semaphore_wait(barrier, total - 1)
    send(first, 0, True)
    loads[3].start()
    for pos in (1, 4, 5):
        loads[pos].wait()
    for c in range(3):
        value = base[c]
        both = by_left(0, 128, value)
        slopes[0, c] = both[:64]
        slopes[1, c] = both[64:]
        slopes[2, c] = by_right(0, 1, value)[0]
    for c, value in enumerate(receive(3, 0, True)):
        state[c] = value * rmult

    sums = []
    for c in range(3):
        value = state[c]
        products = by_left(0, 192, value)
        along, diffuse = by_right(0, 2, value)
        change = products[128:] + diffuse
        for j, slope in enumerate((products[:64], products[64:128], along)):
            change = change + base[j] * slope + state[j] * slopes[j, c]
        sums.append(change)
    send(sums, 1, True)
    for c, value in enumerate(receive(3, 1, True)):
        star[c] = state[c] - time_step * (value * rmult)

    divergence = (
        by_left(0, 64, star[0]) + by_left(64, 128, star[1]) + by_right(0, 1, star[2])[0]
    )
    source[...] = divergence
    for pos in (2, 6, 7, 8):
        loads[pos].wait()

    def coarse_copies(sweep):
        for pos, dx in enumerate((-1, 0, 1)):
            def to(step, carry, dx=dx, pos=pos):
                copy = pltpu.make_async_remote_copy(
                    src_ref=coarse_s.at[sweep],
                    dst_ref=coarse_r.at[sweep, 2 - pos, gy],
                    send_sem=csend.at[sweep, pos],
                    recv_sem=crecv.at[sweep, 2 - pos],
                    device_id=(gx + dx, lax.rem(gy + step, count_y)),
                    device_id_type=MESH,
                )
                copy.start()
                return carry

            if dx == 0:
                lax.fori_loop(1, count_y, to, 0, unroll=True)
            else:
                @pl.when(there(dx, 0))
                def _():
                    lax.fori_loop(0, count_y, to, 0, unroll=True)

    def coarse_wait(sweep, sems):
        for pos, dx in enumerate((-1, 0, 1)):
            part = coarse_r.at[sweep, pos]
            if dx == 0:
                part = coarse_r.at[sweep, pos, pl.ds(0, count_y - 1)]
            if dx == 0:
                pltpu.make_async_copy(part, part, sems.at[sweep, pos]).wait()
            else:

                @pl.when(there(dx, 0))
                def _():
                    pltpu.make_async_copy(part, part, sems.at[sweep, pos]).wait()

    for sweep in range(SWEEPS):
        if sweep == 0:
            whole = source[...]
        else:
            pressure = phi[...]
            whole = source[...] + by_left(192, 256, pressure) + by_right(2, 3, pressure)[0]
        send([-weight_3[...] * whole], 2 * sweep, False)
        resid = receive(1, 2 * sweep, False)[0]
        shares = functools.reduce(
            lambda a, b: a + b, [(resid * rmult)[8 * j : 8 * j + 8] for j in range(8)]
        )
        shares = dot(jnp.concatenate(split(shares), axis=0), down[...])
        shares = jnp.sum(
            shares[0:8, :width] + shares[8:16, :width] + shares[0:8, width:],
            axis=0, keepdims=True,
        )
        coarse_s[sweep] = shares
        coarse_copies(sweep)
        coarse_r[sweep, 1, gy] = shares
        local = by_left(256, 320, resid)
        local = by_right(3, 4, local)[0] * fields[1]
        local = by_left(320, 384, local)
        local = by_right(4, 5, local)[0]
        send([local], 2 * sweep + 1, False)
        coarse_wait(sweep, crecv)
        parts = []
        for pos in range(3):
            part = spread[0] * coarse_r[sweep, pos, 0]
            for j in range(1, count_y):
                part = part + spread[j] * coarse_r[sweep, pos, j]
            parts.append(part)
        high, low = split(jnp.concatenate(parts, axis=0))
        levels = dot(jnp.concatenate([high, low, high], axis=1), up[...])
        lower, own, upper = levels[0:8], levels[8:16], levels[16:24]
        flat = jnp.concatenate([own + lower] + [own] * 6 + [own + upper], axis=0)
        step_sum = along_z(flat) + receive(1, 2 * sweep + 1, False)[0]
        update = relaxation * step_sum * rmult
        phi[...] = update if sweep == 0 else phi[...] + update

    pressure = phi[...]
    both = by_left(0, 128, pressure)
    send([both[:64], both[64:], by_right(0, 1, pressure)[0]], 2, True)
    source[...] = weight_3[...] * rmult * (1.0 / (8.0 * total * (size_z // 8)))
    loads[3].wait()
    for c, value in enumerate(receive(3, 2, True)):
        star[c] = star[c] - value * rmult

    def fold(value):
        return functools.reduce(
            lambda a, b: a + b, [value[:, 128 * t : 128 * t + 128] for t in range(tiles)]
        )

    def products_of(step, sums):
        c, x = step // 8, lax.rem(step, 8)
        rows = pl.ds(pl.multiple_of(8 * x, 8), 8)
        weighted = star[c, rows, :] * source[rows, :]
        return tuple(
            total_k + fold(basis[k, c, rows, :] * weighted) for k, total_k in enumerate(sums)
        )

    zero = jnp.zeros((8, 128), jnp.float32)
    sums = lax.fori_loop(0, 24, products_of, (zero,) * size_b)
    lane_1 = lax.broadcasted_iota(jnp.int32, (1, 128), 1)

    def all_sum(which, value):
        red_s[which] = value

        def to(step, carry):
            other = lax.rem(me + step, total)
            pltpu.make_async_remote_copy(
                src_ref=red_s.at[which], dst_ref=red_r.at[which, me],
                send_sem=rsend.at[which], recv_sem=rrecv.at[which],
                device_id=(other // count_y, lax.rem(other, count_y)), device_id_type=MESH,
            ).start()
            return carry

        lax.fori_loop(1, total, to, 0)
        red_r[which, me] = value
        if which == 0:
            for round_idx in range(2 * SWEEPS):
                each_copy(round_idx, False, "sent")
        else:
            for round_idx in range(3):
                each_copy(round_idx, True, "sent")
            for sweep in range(SWEEPS):
                coarse_wait(sweep, csend)
        part = red_r.at[which, pl.ds(0, total - 1)]
        pltpu.make_async_copy(part, part, rrecv.at[which]).wait()
        pltpu.make_async_copy(part, part, rsend.at[which]).wait()
        return functools.reduce(lambda a, b: a + b, [red_r[which, j] for j in range(total)])

    own = jnp.zeros((1, 128), jnp.float32)
    for k in range(size_b):
        value = jnp.sum(jnp.sum(sums[k], axis=0, keepdims=True), axis=1, keepdims=True)
        own = jnp.where(lane_1 == k, value, own)
    hcol = all_sum(0, own)
    spreads = [
        jnp.broadcast_to(
            jnp.sum(jnp.where(lane_1 == k, hcol, 0.0), axis=1, keepdims=True), (8, 128)
        )
        for k in range(size_b)
    ]

    def remainder_of(step, squares):
        c, x = step // 8, lax.rem(step, 8)
        rows = pl.ds(pl.multiple_of(8 * x, 8), 8)
        for t in range(tiles):
            lanes = slice(128 * t, 128 * t + 128)
            value = star[c, rows, lanes]
            for k in range(size_b):
                value = value - spreads[k] * basis[k, c, rows, lanes]
            star[c, rows, lanes] = value
            squares = squares + value * value * source[rows, lanes]
        return squares

    squares = lax.fori_loop(0, 24, remainder_of, zero)
    store = pltpu.make_async_copy(star, out, load_sem.at[9])
    store.start()
    squared = jnp.sum(jnp.sum(squares, axis=0, keepdims=True), axis=1, keepdims=True)
    squared = all_sum(1, jnp.broadcast_to(squared, (1, 128)))
    beta = jnp.sqrt(squared + norm_eps)
    hess[...] = jnp.where(lane_1 == size_b, beta, hcol)
    norm[...] = jnp.broadcast_to(beta[:, 0:1], norm.shape)
    store.wait()


def per_device(basis, base_flow):
    size_b = basis.shape[0]
    components, size_x, size_y, size_z = base_flow.shape
    count_x = lax.axis_size("gx")
    count_y = lax.axis_size("gy")
    tables = build_tables(count_x, count_y, size_z)
    lanes = tables[5].shape[3]
    vmem = functools.partial(pltpu.VMEM, dtype=jnp.float32)
    dma = pltpu.SemaphoreType.DMA
    exchange = []
    for rounds, comps in ((3, 3), (2 * SWEEPS, 1)):
        shapes = [
            (rounds, 2, comps, 8, size_z),
            (rounds, 2, comps, 8, size_z),
            (rounds, 4, comps, 1, size_z),
        ]
        exchange += [vmem(shape) for shape in shapes * 2]
    spec_v = pl.BlockSpec(memory_space=pltpu.VMEM)
    spec_any = pl.BlockSpec(memory_space=pl.ANY)
    out, hess, norm = pl.pallas_call(
        functools.partial(kernel, count_x, count_y, size_b, size_z),
        out_shape=(
            jax.ShapeDtypeStruct((3, 64, size_z), jnp.float32),
            jax.ShapeDtypeStruct((1, 128), jnp.float32),
            jax.ShapeDtypeStruct((1, size_z), jnp.float32),
        ),
        in_specs=[spec_any] * 8,
        out_specs=(spec_any, spec_v, spec_v),
        scratch_shapes=[
            vmem((size_b, 3, 64, size_z)),
            vmem((3, 64, size_z)),
        ]
        + [pltpu.VMEM(table.shape, table.dtype) for table in tables[:5]]
        + [
            vmem((3, 3, 64, size_z)),
            vmem((count_y, 8, lanes)),
            vmem((3, size_z // 128, 64, 128)),
            vmem((3, 64, size_z)),
            vmem((64, size_z)),
            vmem((64, size_z)),
            vmem((3, 64, size_z)),
        ]
        + exchange
        + [
            vmem((SWEEPS, 1, lanes)),
            vmem((SWEEPS, 3, count_y, 1, lanes)),
            vmem((2, 1, 128)),
            vmem((2, count_x * count_y, 1, 128)),
            dma((10,)),
            dma((3, 8)),
            dma((3, 8)),
            dma((2 * SWEEPS, 8)),
            dma((2 * SWEEPS, 8)),
            dma((SWEEPS, 3)),
            dma((SWEEPS, 3)),
            dma((2,)),
            dma((2,)),
        ],
        compiler_params=pltpu.CompilerParams(
            collective_id=0, has_side_effects=True, vmem_limit_bytes=60 * 1024 * 1024
        ),
    )(
        basis.reshape(size_b, 3, 64, size_z),
        base_flow.reshape(3, 64, size_z),
        *[jnp.asarray(table) for table in tables],
    )
    return (out.reshape(base_flow.shape) / norm[0], hess[0, : size_b + 1])


def solution(mesh):
    return jax.shard_map(
        per_device,
        mesh=mesh,
        in_specs=(P(None, None, "gx", "gy", None), P(None, "gx", "gy", None)),
        out_specs=(P(None, "gx", "gy", None), P()),
        check_vma=False,
    )
```
